512 devices in a mesh: gx: 32 (over z, x), gy: 16 (over y, core).
Axes of the slice: x: 4, y: 8, z: 8, core: 2. Of those that a mesh axis runs over, the one named last changes fastest.
Arguments:
- rhs_field: float32 [256, 128, 128], P('gx', 'gy'), may hold values from -6 to 6
- accumulation: float32 [256, 128, 128], P('gx', 'gy'), may hold values from 0.05 to 0.5
- trans_x: float32 [256, 128, 128], P('gx', 'gy'), may hold values from 0.1 to 10
- trans_y: float32 [256, 128, 128], P('gx', 'gy'), may hold values from 0.1 to 10
- trans_z: float32 [256, 128, 128], P('gx', 'gy'), may hold values from 0.02 to 2
- held_cells: int32 [4, 32, 32, 128], P(None, 'gx', 'gy'), may hold values from 0 to 8191
- perf_host: int32 [32, 32, 128], P('gx', 'gy'), may hold values from 0 to 3, as said below
- well_index: float32 [32, 32, 128], P('gx', 'gy'), may hold values from 0.1 to 2
- seg_cond: float32 [32, 32, 128], P('gx', 'gy'), may hold values from 0.5 to 4
- seg_rate: float32 [32, 32, 128], P('gx', 'gy'), may hold values from -6 to 6
Outputs:
- pressure: float32 [256, 128, 128], P('gx', 'gy')
- seg_pressure: float32 [32, 32, 128], P('gx', 'gy')
The draws below stay inside these ranges and needn't reach their ends.
Inputs may be any that keep to these rules, and one draw needn't show every extreme that they name: `held_cells`: local cell numbers, x-major then y then layer. `perf_host`: nondecreasing along a well's slots, starting at 0 in slot 0 and ending at 3 in the last slot: the perforations on each device form one run of slots.
All inputs are finite; a program needn't handle non-finite values.
Results may differ from the reference program's by a relative error of at most 0.00002.
Values sent between devices are 32-bit elements; how exact they have to be, the bound alone decides.
No kernel may reach another device: no remote copies, remote signals or barrier semaphores. Data moves between devices by JAX's collectives and lax.ppermute only.
A program may use at most 64 MiB of HBM per device.

```python
import math
import jax
import jax.numpy as jnp

CX = 8
CY = 8
CZ = 128
W_DEV = 2
PERF = 128
REACH = 4
SWEEPS = 6
NX = 256
NY = 128
WROWS = 32
N_GX = 32
N_GY = 16


def draw_perf_host(key, part):
    cuts = jax.random.randint(key, (N_GX, WROWS, REACH - 1), 1, PERF)
    slot = jnp.arange(PERF, dtype=jnp.int32)
    above = (slot[None, None, None, :] >= cuts[:, :, :, None]).astype(jnp.int32)
    return jnp.sum(above, axis=2).astype(jnp.int32)


def touch_ends(result, stream_key, low, top_value):
    extent = result.shape
    index_at = [jax.random.randint(jax.random.fold_in(stream_key, axis), (), 0, extent[axis]) for axis in range(len(extent))]
    result = result.at[tuple(index_at)].set(low)
    longest = extent.index(max(extent))
    index_at[longest] = (index_at[longest] + 1) % extent[longest]
    return result.at[tuple(index_at)].set(top_value)


def level_of(own_key, dims, split, low, top_value):
    def one(axis_at, parts):
        steps = jax.random.uniform(jax.random.fold_in(jax.random.fold_in(own_key, 6), axis_at), (parts,), jnp.float32, low / len(split), top_value / len(split))
        return jnp.repeat(jnp.exp(steps), dims[axis_at] // parts).reshape((-1,) + (1,) * (len(dims) - axis_at - 1))

    factor_of = one(*split[0])
    for cut in split[1:]:
        factor_of = factor_of * one(*cut)
    return factor_of


def noise(rng, dims, spread, most, pieces=(), kind=jnp.bfloat16):
    values = spread * jax.random.normal(rng, dims, jnp.float32)
    if pieces:
        values = values * level_of(rng, dims, pieces, -0.22, 0.18)
    return jnp.clip(values, -most, most).astype(kind)


def setup_inputs(seed: int = 0) -> dict:
    keys = jax.random.split(jax.random.key(seed), 11)
    rhs_field = noise(keys[0], (NX, NY, CZ), 1.0, 6.0, ((0, 32), (1, 16)), jnp.float32)
    accumulation = jnp.clip(jnp.exp(math.log(0.5) - 2.3025851 * jax.random.uniform(keys[1], (NX, NY, CZ), jnp.float32) ** level_of(keys[1], (NX, NY, CZ), ((0, 32), (1, 16)), -0.2, 0.2)), 0.05, 0.5)
    trans_x = jnp.clip(jnp.exp(math.log(10.0) - 4.6051702 * jax.random.uniform(keys[2], (NX, NY, CZ), jnp.float32) ** level_of(keys[2], (NX, NY, CZ), ((0, 32), (1, 16)), -0.2, 0.2)), 0.1, 10.0)
    trans_y = jnp.clip(jnp.exp(math.log(10.0) - 4.6051702 * jax.random.uniform(keys[3], (NX, NY, CZ), jnp.float32) ** level_of(keys[3], (NX, NY, CZ), ((0, 32), (1, 16)), -0.2, 0.2)), 0.1, 10.0)
    trans_z = jnp.clip(jnp.exp(math.log(2.0) - 4.6051702 * jax.random.uniform(keys[4], (NX, NY, CZ), jnp.float32) ** level_of(keys[4], (NX, NY, CZ), ((0, 32), (1, 16)), -0.2, 0.2)), 0.02, 2.0)
    held_cells = touch_ends(jax.random.randint(keys[5], (REACH, N_GX, WROWS, PERF), 0, CX * CY * CZ), jax.random.fold_in(keys[5], 1), 0, (CX * CY * CZ) - 1).astype(jnp.int32)
    perf_host = draw_perf_host(jax.random.fold_in(keys[10], 71), 0)
    well_index = jnp.clip(jnp.exp(math.log(2.0) - 2.9957323 * jax.random.uniform(keys[7], (N_GX, WROWS, PERF), jnp.float32) ** level_of(keys[7], (N_GX, WROWS, PERF), ((0, 32), (1, 16)), -0.2, 0.2)), 0.1, 2.0)
    seg_cond = jnp.clip(jnp.exp(math.log(4.0) - 2.0794415 * jax.random.uniform(keys[8], (N_GX, WROWS, PERF), jnp.float32) ** level_of(keys[8], (N_GX, WROWS, PERF), ((0, 32), (1, 16)), -0.2, 0.2)), 0.5, 4.0)
    seg_rate = noise(keys[9], (N_GX, WROWS, PERF), 1.0, 6.0, ((0, 32), (1, 16)), jnp.float32)
    return {"rhs_field": rhs_field, "accumulation": accumulation, "trans_x": trans_x, "trans_y": trans_y, "trans_z": trans_z, "held_cells": held_cells, "perf_host": perf_host, "well_index": well_index, "seg_cond": seg_cond, "seg_rate": seg_rate}


def moved_up(field, axis):
    size = field.shape[axis]
    head = jnp.zeros_like(jax.lax.slice_in_dim(field, 0, 1, axis=axis))
    return jnp.concatenate([head, jax.lax.slice_in_dim(field, 0, size - 1, axis=axis)], axis=axis)


def to_local(field):
    return field.reshape(N_GX, CX, N_GY, CY, CZ).transpose(0, 2, 1, 3, 4).reshape(N_GX, N_GY, CX * CY * CZ)


def from_local(blocks):
    return blocks.reshape(N_GX, N_GY, CX, CY, CZ).transpose(0, 2, 1, 3, 4).reshape(NX, NY, CZ)


def reference(rhs_field, accumulation, trans_x, trans_y, trans_z, held_cells, perf_host, well_index, seg_cond, seg_rate):
    wx = moved_up(trans_x, 0)
    wy = moved_up(trans_y, 1)
    wz = moved_up(trans_z, 2)
    diag = accumulation + trans_x + wx + trans_y + wy + trans_z + wz
    slot = jnp.arange(PERF)
    fm = jnp.where(slot[None, None, :] > 0, seg_cond, jnp.float32(0.0))
    fp = jnp.concatenate([fm[:, :, 1:], jnp.zeros_like(fm[:, :, :1])], axis=2)
    held = held_cells.reshape(REACH, N_GX, N_GY, W_DEV * PERF)
    pressure = jnp.zeros_like(rhs_field)
    seg_pressure = jnp.zeros_like(seg_rate)
    row_x = jnp.arange(N_GX)[:, None, None]
    row_y = jnp.arange(N_GY)[None, :, None]
    for sweep in range(SWEEPS):
        blocks = to_local(pressure)
        cell_p = jnp.zeros_like(seg_rate)
        for r in range(REACH):
            values = jnp.take_along_axis(blocks, held[r], axis=2).reshape(N_GX, WROWS, PERF)
            values = jnp.roll(values, -r, axis=0)
            cell_p = cell_p + jnp.where(perf_host == r, values, jnp.float32(0.0))
        seg_prev = jnp.concatenate([jnp.zeros_like(seg_pressure[:, :, :1]), seg_pressure[:, :, :-1]], axis=2)
        seg_next = jnp.concatenate([seg_pressure[:, :, 1:], jnp.zeros_like(seg_pressure[:, :, :1])], axis=2)
        seg_res = seg_rate - (well_index * (seg_pressure - cell_p) + fm * (seg_pressure - seg_prev) + fp * (seg_pressure - seg_next))
        seg_pressure = seg_pressure + 0.8 * seg_res / (well_index + fm + fp)
        flux = well_index * (cell_p - seg_pressure)
        term_blocks = jnp.zeros_like(blocks)
        for r in range(REACH):
            sent = jnp.roll(jnp.where(perf_host == r, flux, jnp.float32(0.0)), r, axis=0)
            term_blocks = term_blocks.at[row_x, row_y, held[r]].add(sent.reshape(N_GX, N_GY, W_DEV * PERF))
        well_term = from_local(term_blocks)
        padded = jnp.pad(pressure, 1)
        core = padded[1:-1, 1:-1, 1:-1]
        applied = accumulation * pressure
        applied = applied + trans_x * (core - padded[2:, 1:-1, 1:-1]) + wx * (core - padded[:-2, 1:-1, 1:-1])
        applied = applied + trans_y * (core - padded[1:-1, 2:, 1:-1]) + wy * (core - padded[1:-1, :-2, 1:-1])
        applied = applied + trans_z * (core - padded[1:-1, 1:-1, 2:]) + wz * (core - padded[1:-1, 1:-1, :-2])
        pressure = pressure + 0.7 * (rhs_field - applied - well_term) / diag
    return pressure, seg_pressure
```

```python
import jax
import jax.numpy as jnp
from jax import lax
from jax.experimental import pallas as pl
from jax.experimental.pallas import tpu as pltpu
from jax.sharding import PartitionSpec as P

SWEEPS = 6
F32 = jnp.float32
BF16 = jnp.bfloat16


def split3(value):
    high = value.astype(BF16)
    rest = value - high.astype(F32)
    middle = rest.astype(BF16)
    low = (rest - middle.astype(F32)).astype(BF16)
    return high, middle, low


def iota(shape, dim):
    return lax.broadcasted_iota(jnp.int32, shape, dim)


def lane_onehot(idx, lanes):
    lane_of = idx & (lanes - 1)
    pieces = []
    for row in range(idx.shape[0]):
        hit = iota((lanes, idx.shape[1]), 0) == lane_of[row : row + 1, :]
        pieces.append(jnp.where(hit, F32(1.0), F32(0.0)).astype(BF16))
    return jnp.concatenate(pieces, axis=1)


def row_hit(idx, row, lanes, count):
    shift = lanes.bit_length() - 1
    row_of = lax.shift_right_logical(idx[row : row + 1, :], shift)
    return iota((count, idx.shape[1]), 0) == row_of


def scatter(flux, idx, lane_hot, count, lanes):
    parts = [part.astype(F32) for part in split3(flux)]
    columns = []
    for row in range(idx.shape[0]):
        hit = row_hit(idx, row, lanes, count)
        columns.append(
            jnp.concatenate(
                [jnp.where(hit, part[row : row + 1, :], F32(0.0)).astype(BF16) for part in parts],
                axis=0,
            )
        )
    spread = jnp.concatenate(columns, axis=1)
    out = lax.dot_general(
        spread, lane_hot, (((1,), (1,)), ((), ())), preferred_element_type=F32
    )
    return out[:count] + out[count : 2 * count] + out[2 * count :]


def gather(cells, idx, lane_hot, lanes):
    count = cells.shape[0]
    stacked = jnp.concatenate(split3(cells), axis=0)
    picked = lax.dot_general(
        stacked, lane_hot, (((1,), (0,)), ((), ())), preferred_element_type=F32
    )
    picked = picked[:count] + picked[count : 2 * count] + picked[2 * count :]
    slots = idx.shape[1]
    out = jnp.zeros(idx.shape, F32)
    for row in range(idx.shape[0]):
        part = jnp.where(
            row_hit(idx, row, lanes, count), picked[:, row * slots : (row + 1) * slots], F32(0.0)
        )
        total = jnp.sum(part, axis=0, keepdims=True)
        out = jnp.where(iota(idx.shape, 0) == row, total, out)
    return out


def well_update(rate, index, fm, seg, cell_p):
    slots = seg.shape[1]
    fp = pltpu.roll(fm, slots - 1, 1)
    seg_prev = pltpu.roll(seg, 1, 1)
    seg_next = pltpu.roll(seg, slots - 1, 1)
    seg_res = rate - (
        index * (seg - cell_p) + fm * (seg - seg_prev) + fp * (seg - seg_next)
    )
    return seg + F32(0.8) * seg_res / (index + fm + fp)


def y_shifted(block, edge, step):
    planes = []
    size = block.shape[1]
    for x in range(block.shape[0]):
        moved = pltpu.roll(block[x], (-step) % size, 0)
        at = size - 1 if step > 0 else 0
        planes.append(jnp.where(iota(moved.shape, 0) == at, edge[x : x + 1, :], moved))
    return planes


def z_shifted(plane, step):
    size = plane.shape[1]
    moved = pltpu.roll(plane, (-step) % size, 1)
    at = size - 1 if step > 0 else 0
    return jnp.where(iota(plane.shape, 1) == at, F32(0.0), moved)


def send_out(pos, ring, vals, p, send_ref, ylo_ref, yhi_ref, reach):
    width = p.shape[0]
    rows = vals.shape[0]
    send_ref[...] = jnp.zeros(send_ref.shape, F32)
    for d in range(1 - reach, reach):
        send_ref[lax.rem(pos + d + ring, ring), :rows, :] = vals
    send_ref[lax.rem(pos + 1, ring), rows:, :] = p[width - 1]
    send_ref[lax.rem(pos + ring - 1, ring), rows:, :] = p[0]
    for x in range(width):
        ylo_ref[x : x + 1, :] = p[x][:1, :]
        yhi_ref[x : x + 1, :] = p[x][-1:, :]


def pack_kernel(pos_ref, tx_ref, ty_ref, host_ref, index_ref, cond_ref, rate_ref, send_ref, yhi_ref, *, reach):
    pos = pos_ref[0]
    ring = send_ref.shape[0]
    width = tx_ref.shape[0]
    pack = jnp.concatenate(
        [host_ref[0].astype(F32), index_ref[0], cond_ref[0], rate_ref[0]], axis=0
    )
    rows = pack.shape[0]
    send_ref[...] = jnp.zeros(send_ref.shape, F32)
    for d in range(reach):
        send_ref[lax.rem(pos + d, ring), :rows, :] = pack
    send_ref[lax.rem(pos + 1, ring), rows:, :] = tx_ref[width - 1]
    for x in range(width):
        yhi_ref[x : x + 1, :] = ty_ref[x, ty_ref.shape[1] - 1 :, :]


def first_kernel(
    pos_ref, rhs_ref, acc_ref, tx_ref, ty_ref, tz_ref, recv_ref, wy_ref, held_ref,
    p_ref, gain_ref, wx_ref, seg_ref, well_ref, send_ref, ylo_ref, yhi_ref, *, reach, wells,
):
    pos = pos_ref[0]
    ring = recv_ref.shape[0]
    width, depth, lanes = rhs_ref.shape
    rows = reach * wells
    slots = lanes
    groups = []
    for array in range(4):
        whole = jnp.zeros((rows, slots), F32)
        for q in range(reach):
            piece = recv_ref[lax.rem(pos + ring - q, ring), :rows, :]
            moved = pltpu.roll(piece, (wells * (q - array)) % rows, 0) if q != array else piece
            whole = jnp.where(iota((rows, slots), 0) // wells == q, moved, whole)
        groups.append(whole)
    host, index, cond, rate = groups
    fm = jnp.where(iota((rows, slots), 1) > 0, cond, F32(0.0))
    well_ref[0], well_ref[1], well_ref[2], well_ref[3] = host, index, fm, rate
    zero = jnp.zeros((rows, slots), F32)
    seg = well_update(rate, index, fm, zero, zero)
    seg_ref[...] = seg
    flux = F32(0.0) - index * seg
    idx = held_ref[...].reshape(rows, slots)
    own = (iota((rows, slots), 0) // wells).astype(F32)
    flux = jnp.where(host == own, flux, F32(0.0))
    hot = lane_onehot(idx, lanes)
    count = width * depth
    well_term = scatter(flux, idx, hot, count, lanes).reshape(width, depth, lanes)
    west = jnp.where(pos == 0, F32(0.0), recv_ref[lax.rem(pos + ring - 1, ring), rows:, :])
    wx_ref[...] = west
    wy = y_shifted(ty_ref[...], wy_ref[...], -1)
    planes = []
    for x in range(width):
        tz = tz_ref[x]
        diag = acc_ref[x] + tx_ref[x] + (west if x == 0 else tx_ref[x - 1])
        diag = diag + ty_ref[x] + wy[x] + tz + z_shifted(tz, -1)
        gain = F32(0.7) / diag
        gain_ref[x] = gain
        planes.append(gain * (rhs_ref[x] - well_term[x]))
    for x in range(width):
        p_ref[x] = planes[x]
    cells = jnp.concatenate(planes, axis=0)
    vals = gather(cells, idx, hot, lanes)
    send_out(pos, ring, vals, planes_array(planes), send_ref, ylo_ref, yhi_ref, reach)


class planes_array:
    def __init__(self, planes):
        self.planes = planes
        self.shape = (len(planes), *planes[0].shape)

    def __getitem__(self, x):
        return self.planes[x]


def sweep_kernel(
    pos_ref, p_in, rhs_ref, tx_ref, ty_ref, tz_ref, gain_ref, wx_ref, wy_ref, recv_ref, south_ref, north_ref,
    seg_in, well_ref, held_ref, p_ref, seg_ref, *rest, reach, wells, last,
):
    pos = pos_ref[0]
    ring = recv_ref.shape[0]
    width, depth, lanes = rhs_ref.shape
    rows = reach * wells
    slots = lanes
    host, index, fm, rate = well_ref[0], well_ref[1], well_ref[2], well_ref[3]
    own_row = iota((rows, slots), 0) // wells
    cell_p = jnp.zeros((rows, slots), F32)
    for d in range(1 - reach, reach):
        piece = recv_ref[lax.rem(pos + d + ring, ring), :rows, :]
        moved = pltpu.roll(piece, (-wells * d) % rows, 0) if d else piece
        cell_p = jnp.where(host == (own_row + d).astype(F32), moved, cell_p)
    seg = well_update(rate, index, fm, seg_in[...], cell_p)
    if last:
        seg_ref[0] = seg[:wells]
    else:
        seg_ref[...] = seg
    flux = index * (cell_p - seg)
    flux = jnp.where(host == own_row.astype(F32), flux, F32(0.0))
    idx = held_ref[...].reshape(rows, slots)
    hot = lane_onehot(idx, lanes)
    count = width * depth
    well_term = scatter(flux, idx, hot, count, lanes).reshape(width, depth, lanes)
    west = jnp.where(pos == 0, F32(0.0), recv_ref[lax.rem(pos + ring - 1, ring), rows:, :])
    east = jnp.where(pos == ring - 1, F32(0.0), recv_ref[lax.rem(pos + 1, ring), rows:, :])
    block = p_in[...]
    wy = y_shifted(ty_ref[...], wy_ref[...], -1)
    south = y_shifted(block, south_ref[...], -1)
    north = y_shifted(block, north_ref[...], 1)
    planes = []
    for x in range(width):
        tz = tz_ref[x]
        total = rhs_ref[x] - well_term[x]
        total = total + tx_ref[x] * (east if x == width - 1 else block[x + 1])
        total = total + (wx_ref[...] * west if x == 0 else tx_ref[x - 1] * block[x - 1])
        total = total + ty_ref[x] * north[x] + wy[x] * south[x]
        total = total + tz * z_shifted(block[x], 1) + z_shifted(tz, -1) * z_shifted(block[x], -1)
        planes.append(F32(0.3) * block[x] + gain_ref[x] * total)
    for x in range(width):
        p_ref[x] = planes[x]
    if not last:
        send_ref, ylo_ref, yhi_ref = rest
        vals = gather(jnp.concatenate(planes, axis=0), idx, hot, lanes)
        send_out(pos, ring, vals, planes_array(planes), send_ref, ylo_ref, yhi_ref, reach)


def shards(
    rhs_field,
    accumulation,
    trans_x,
    trans_y,
    trans_z,
    held_cells,
    perf_host,
    well_index,
    seg_cond,
    seg_rate,
):
    width, depth, layers = rhs_field.shape
    reach = held_cells.shape[0]
    wells = well_index.shape[1]
    slots = well_index.shape[2]
    rows = reach * wells
    ring = lax.axis_size("gx")
    county = lax.axis_size("gy")
    up = [(j, j + 1) for j in range(county - 1)]
    down = [(target, source) for source, target in up]
    pos = lax.axis_index("gx").astype(jnp.int32).reshape(1)

    def shape(*dims):
        return jax.ShapeDtypeStruct(dims, F32)

    smem = pl.BlockSpec(memory_space=pltpu.SMEM)
    vmem = pl.BlockSpec(memory_space=pltpu.VMEM)

    def call(body, outs, *args, **static):
        return pl.pallas_call(
            lambda *refs: body(*refs, **static),
            out_shape=outs,
            in_specs=[smem] + [vmem] * (len(args) - 1),
            out_specs=[vmem] * len(outs),
        )(*args)

    message = shape(ring, rows + depth, slots)
    edge = shape(width, layers)
    block = shape(width, depth, layers)

    def exchanged(send):
        return lax.all_to_all(send, "gx", 0, 0, tiled=True)

    send, yhi = call(
        pack_kernel, [message, edge], pos, trans_x, trans_y, perf_host, well_index, seg_cond, seg_rate,
        reach=reach,
    )
    wy = lax.ppermute(yhi, "gy", up)
    recv = exchanged(send)
    p, gain, wx, seg, well, send, ylo, yhi = call(
        first_kernel,
        [block, block, shape(depth, layers), shape(rows, slots), shape(4, rows, slots), message, edge, edge],
        pos, rhs_field, accumulation, trans_x, trans_y, trans_z, recv, wy, held_cells,
        reach=reach, wells=wells,
    )
    for sweep in range(1, SWEEPS):
        last = sweep == SWEEPS - 1
        south = lax.ppermute(yhi, "gy", up)
        north = lax.ppermute(ylo, "gy", down)
        recv = exchanged(send)
        outs = [block, shape(1, wells, slots) if last else shape(rows, slots)]
        if not last:
            outs += [message, edge, edge]
        got = call(
            sweep_kernel, outs, pos, p, rhs_field, trans_x, trans_y, trans_z, gain, wx, wy, recv, south, north,
            seg, well, held_cells, reach=reach, wells=wells, last=last,
        )
        p, seg = got[:2]
        if not last:
            send, ylo, yhi = got[2:]
    return (p, seg)


def solution(mesh):
    return jax.shard_map(
        shards,
        mesh=mesh,
        in_specs=(
            P("gx", "gy", None),
            P("gx", "gy", None),
            P("gx", "gy", None),
            P("gx", "gy", None),
            P("gx", "gy", None),
            P(None, "gx", "gy", None),
            P("gx", "gy", None),
            P("gx", "gy", None),
            P("gx", "gy", None),
            P("gx", "gy", None),
        ),
        out_specs=(P("gx", "gy", None), P("gx", "gy", None)),
        check_vma=False,
    )
```

```python
import jax
import jax.numpy as jnp
from jax import lax
from jax.experimental import pallas as pl
from jax.experimental.pallas import tpu as pltpu
from jax.sharding import PartitionSpec as P

SWEEPS = 6
F32 = jnp.float32
BF16 = jnp.bfloat16


def split3(value):
    high = value.astype(BF16)
    rest = value - high.astype(F32)
    middle = rest.astype(BF16)
    low = (rest - middle.astype(F32)).astype(BF16)
    return high, middle, low


def iota(shape, dim):
    return lax.broadcasted_iota(jnp.int32, shape, dim)


def lane_onehot(idx, lanes):
    lane_of = idx & (lanes - 1)
    pieces = []
    for row in range(idx.shape[0]):
        hit = iota((lanes, idx.shape[1]), 0) == lane_of[row : row + 1, :]
        pieces.append(jnp.where(hit, F32(1.0), F32(0.0)).astype(BF16))
    return jnp.concatenate(pieces, axis=1)


def row_hit(idx, row, lanes, count):
    shift = lanes.bit_length() - 1
    row_of = lax.shift_right_logical(idx[row : row + 1, :], shift)
    return iota((count, idx.shape[1]), 0) == row_of


def scatter(flux, idx, lane_hot, count, lanes):
    parts = [part.astype(F32) for part in split3(flux)]
    columns = []
    for row in range(idx.shape[0]):
        hit = row_hit(idx, row, lanes, count)
        columns.append(
            jnp.concatenate(
                [jnp.where(hit, part[row : row + 1, :], F32(0.0)).astype(BF16) for part in parts],
                axis=0,
            )
        )
    spread = jnp.concatenate(columns, axis=1)
    out = lax.dot_general(
        spread, lane_hot, (((1,), (1,)), ((), ())), preferred_element_type=F32
    )
    return out[:count] + out[count : 2 * count] + out[2 * count :]


def gather(cells, idx, lane_hot, lanes):
    count = cells.shape[0]
    stacked = jnp.concatenate(split3(cells), axis=0)
    picked = lax.dot_general(
        stacked, lane_hot, (((1,), (0,)), ((), ())), preferred_element_type=F32
    )
    picked = picked[:count] + picked[count : 2 * count] + picked[2 * count :]
    slots = idx.shape[1]
    out = jnp.zeros(idx.shape, F32)
    for row in range(idx.shape[0]):
        part = jnp.where(
            row_hit(idx, row, lanes, count), picked[:, row * slots : (row + 1) * slots], F32(0.0)
        )
        total = jnp.sum(part, axis=0, keepdims=True)
        out = jnp.where(iota(idx.shape, 0) == row, total, out)
    return out


def well_update(rate, index, fm, seg, cell_p):
    slots = seg.shape[1]
    fp = pltpu.roll(fm, slots - 1, 1)
    seg_prev = pltpu.roll(seg, 1, 1)
    seg_next = pltpu.roll(seg, slots - 1, 1)
    seg_res = rate - (
        index * (seg - cell_p) + fm * (seg - seg_prev) + fp * (seg - seg_next)
    )
    return seg + F32(0.8) * seg_res / (index + fm + fp)


def y_shifted(block, edge, step):
    planes = []
    size = block.shape[1]
    for x in range(block.shape[0]):
        moved = pltpu.roll(block[x], (-step) % size, 0)
        at = size - 1 if step > 0 else 0
        planes.append(jnp.where(iota(moved.shape, 0) == at, edge[x : x + 1, :], moved))
    return planes


def z_shifted(plane, step):
    size = plane.shape[1]
    moved = pltpu.roll(plane, (-step) % size, 1)
    at = size - 1 if step > 0 else 0
    return jnp.where(iota(plane.shape, 1) == at, F32(0.0), moved)


def send_out(pos, ring, vals, p, send_ref, ylo_ref, yhi_ref, reach):
    width = p.shape[0]
    rows = vals.shape[0]
    send_ref[...] = jnp.zeros(send_ref.shape, F32)
    for d in range(1 - reach, reach):
        send_ref[lax.rem(pos + d + ring, ring), :rows, :] = vals
    send_ref[lax.rem(pos + 1, ring), rows:, :] = p[width - 1]
    send_ref[lax.rem(pos + ring - 1, ring), rows:, :] = p[0]
    for x in range(width):
        ylo_ref[x : x + 1, :] = p[x][:1, :]
        yhi_ref[x : x + 1, :] = p[x][-1:, :]


def pack_kernel(pos_ref, tx_ref, ty_ref, host_ref, index_ref, cond_ref, rate_ref, send_ref, yhi_ref, *, reach):
    pos = pos_ref[0]
    ring = send_ref.shape[0]
    width = tx_ref.shape[0]
    pack = jnp.concatenate(
        [host_ref[0].astype(F32), index_ref[0], cond_ref[0], rate_ref[0]], axis=0
    )
    rows = pack.shape[0]
    send_ref[...] = jnp.zeros(send_ref.shape, F32)
    for d in range(reach):
        send_ref[lax.rem(pos + d, ring), :rows, :] = pack
    send_ref[lax.rem(pos + 1, ring), rows:, :] = tx_ref[width - 1]
    for x in range(width):
        yhi_ref[x : x + 1, :] = ty_ref[x, ty_ref.shape[1] - 1 :, :]


def first_kernel(
    pos_ref, rhs_ref, acc_ref, tx_ref, ty_ref, tz_ref, recv_ref, wy_ref, held_ref,
    p_ref, gain_ref, wx_ref, seg_ref, well_ref, send_ref, ylo_ref, yhi_ref, *, reach, wells,
):
    pos = pos_ref[0]
    ring = recv_ref.shape[0]
    width, depth, lanes = rhs_ref.shape
    rows = reach * wells
    slots = lanes
    groups = []
    for array in range(4):
        whole = jnp.zeros((rows, slots), F32)
        for q in range(reach):
            piece = recv_ref[lax.rem(pos + ring - q, ring), :rows, :]
            moved = pltpu.roll(piece, (wells * (q - array)) % rows, 0) if q != array else piece
            whole = jnp.where(iota((rows, slots), 0) // wells == q, moved, whole)
        groups.append(whole)
    host, index, cond, rate = groups
    fm = jnp.where(iota((rows, slots), 1) > 0, cond, F32(0.0))
    well_ref[0], well_ref[1], well_ref[2], well_ref[3] = host, index, fm, rate
    zero = jnp.zeros((rows, slots), F32)
    seg = well_update(rate, index, fm, zero, zero)
    seg_ref[...] = seg
    flux = F32(0.0) - index * seg
    idx = held_ref[...].reshape(rows, slots)
    own = (iota((rows, slots), 0) // wells).astype(F32)
    flux = jnp.where(host == own, flux, F32(0.0))
    hot = lane_onehot(idx, lanes)
    count = width * depth
    well_term = scatter(flux, idx, hot, count, lanes).reshape(width, depth, lanes)
    west = jnp.where(pos == 0, F32(0.0), recv_ref[lax.rem(pos + ring - 1, ring), rows:, :])
    wx_ref[...] = west
    wy = y_shifted(ty_ref[...], wy_ref[...], -1)
    planes = []
    for x in range(width):
        tz = tz_ref[x]
        diag = acc_ref[x] + tx_ref[x] + (west if x == 0 else tx_ref[x - 1])
        diag = diag + ty_ref[x] + wy[x] + tz + z_shifted(tz, -1)
        gain = F32(0.7) / diag
        gain_ref[x] = gain
        planes.append(gain * (rhs_ref[x] - well_term[x]))
    for x in range(width):
        p_ref[x] = planes[x]
    cells = jnp.concatenate(planes, axis=0)
    vals = gather(cells, idx, hot, lanes)
    send_out(pos, ring, vals, planes_array(planes), send_ref, ylo_ref, yhi_ref, reach)


class planes_array:
    def __init__(self, planes):
        self.planes = planes
        self.shape = (len(planes), *planes[0].shape)

    def __getitem__(self, x):
        return self.planes[x]


def sweep_kernel(
    pos_ref, p_in, rhs_ref, tx_ref, ty_ref, tz_ref, gain_ref, wx_ref, wy_ref, recv_ref, south_ref, north_ref,
    seg_in, well_ref, held_ref, p_ref, seg_ref, *rest, reach, wells, last,
):
    pos = pos_ref[0]
    ring = recv_ref.shape[0]
    width, depth, lanes = rhs_ref.shape
    rows = reach * wells
    slots = lanes
    host, index, fm, rate = well_ref[0], well_ref[1], well_ref[2], well_ref[3]
    own_row = iota((rows, slots), 0) // wells
    cell_p = jnp.zeros((rows, slots), F32)
    for d in range(1 - reach, reach):
        piece = recv_ref[lax.rem(pos + d + ring, ring), :rows, :]
        moved = pltpu.roll(piece, (-wells * d) % rows, 0) if d else piece
        cell_p = jnp.where(host == (own_row + d).astype(F32), moved, cell_p)
    seg = well_update(rate, index, fm, seg_in[...], cell_p)
    if last:
        seg_ref[0] = seg[:wells]
    else:
        seg_ref[...] = seg
    flux = index * (cell_p - seg)
    flux = jnp.where(host == own_row.astype(F32), flux, F32(0.0))
    idx = held_ref[...].reshape(rows, slots)
    hot = lane_onehot(idx, lanes)
    count = width * depth
    well_term = scatter(flux, idx, hot, count, lanes).reshape(width, depth, lanes)
    west = jnp.where(pos == 0, F32(0.0), recv_ref[lax.rem(pos + ring - 1, ring), rows:, :])
    east = jnp.where(pos == ring - 1, F32(0.0), recv_ref[lax.rem(pos + 1, ring), rows:, :])
    block = p_in[...]
    wy = y_shifted(ty_ref[...], wy_ref[...], -1)
    south = y_shifted(block, south_ref[...], -1)
    north = y_shifted(block, north_ref[...], 1)
    planes = []
    for x in range(width):
        tz = tz_ref[x]
        total = rhs_ref[x] - well_term[x]
        total = total + tx_ref[x] * (east if x == width - 1 else block[x + 1])
        total = total + (wx_ref[...] * west if x == 0 else tx_ref[x - 1] * block[x - 1])
        total = total + ty_ref[x] * north[x] + wy[x] * south[x]
        total = total + tz * z_shifted(block[x], 1) + z_shifted(tz, -1) * z_shifted(block[x], -1)
        planes.append(F32(0.3) * block[x] + gain_ref[x] * total)
    for x in range(width):
        p_ref[x] = planes[x]
    if not last:
        send_ref, ylo_ref, yhi_ref = rest
        vals = gather(jnp.concatenate(planes, axis=0), idx, hot, lanes)
        send_out(pos, ring, vals, planes_array(planes), send_ref, ylo_ref, yhi_ref, reach)


def shards(
    rhs_field,
    accumulation,
    trans_x,
    trans_y,
    trans_z,
    held_cells,
    perf_host,
    well_index,
    seg_cond,
    seg_rate,
):
    width, depth, layers = rhs_field.shape
    reach = held_cells.shape[0]
    wells = well_index.shape[1]
    slots = well_index.shape[2]
    rows = reach * wells
    ring = lax.axis_size("gx")
    county = lax.axis_size("gy")
    up = [(j, j + 1) for j in range(county - 1)]
    down = [(target, source) for source, target in up]
    pos = lax.axis_index("gx").astype(jnp.int32).reshape(1)

    def shape(*dims):
        return pltpu.VMEM(dims, F32)

    def result(*dims):
        return jax.ShapeDtypeStruct(dims, F32)

    def near(value):
        return pltpu.with_memory_space_constraint(value, pltpu.VMEM)

    smem = pl.BlockSpec(memory_space=pltpu.SMEM)
    vmem = pl.BlockSpec(memory_space=pltpu.VMEM)

    def call(body, outs, *args, **static):
        return pl.pallas_call(
            lambda *refs: body(*refs, **static),
            out_shape=outs,
            in_specs=[smem] + [vmem] * (len(args) - 1),
            out_specs=[vmem] * len(outs),
        )(args[0], *map(near, args[1:]))

    message = shape(ring, rows + depth, slots)
    edge = shape(width, layers)
    block = shape(width, depth, layers)

    def exchanged(send):
        return lax.all_to_all(send, "gx", 0, 0, tiled=True)

    send, yhi = call(
        pack_kernel, [message, edge], pos, trans_x, trans_y, perf_host, well_index, seg_cond, seg_rate,
        reach=reach,
    )
    wy = lax.ppermute(yhi, "gy", up)
    recv = exchanged(send)
    p, gain, wx, seg, well, send, ylo, yhi = call(
        first_kernel,
        [block, block, shape(depth, layers), shape(rows, slots), shape(4, rows, slots), message, edge, edge],
        pos, rhs_field, accumulation, trans_x, trans_y, trans_z, recv, wy, held_cells,
        reach=reach, wells=wells,
    )
    for sweep in range(1, SWEEPS):
        last = sweep == SWEEPS - 1
        south = lax.ppermute(yhi, "gy", up)
        north = lax.ppermute(ylo, "gy", down)
        recv = exchanged(send)
        outs = [result(width, depth, layers), result(1, wells, slots)] if last else [block, shape(rows, slots)]
        if not last:
            outs += [message, edge, edge]
        got = call(
            sweep_kernel, outs, pos, p, rhs_field, trans_x, trans_y, trans_z, gain, wx, wy, recv, south, north,
            seg, well, held_cells, reach=reach, wells=wells, last=last,
        )
        p, seg = got[:2]
        if not last:
            send, ylo, yhi = got[2:]
    return (p, seg)


def solution(mesh):
    return jax.shard_map(
        shards,
        mesh=mesh,
        in_specs=(
            P("gx", "gy", None),
            P("gx", "gy", None),
            P("gx", "gy", None),
            P("gx", "gy", None),
            P("gx", "gy", None),
            P(None, "gx", "gy", None),
            P("gx", "gy", None),
            P("gx", "gy", None),
            P("gx", "gy", None),
            P("gx", "gy", None),
        ),
        out_specs=(P("gx", "gy", None), P("gx", "gy", None)),
        check_vma=False,
    )
```

```python
import jax
import jax.numpy as jnp
from jax import lax
from jax.experimental import pallas as pl
from jax.experimental.pallas import tpu as pltpu
from jax.sharding import PartitionSpec as P

SWEEPS = 6
F32 = jnp.float32
BF16 = jnp.bfloat16


def split3(value):
    high = value.astype(BF16)
    rest = value - high.astype(F32)
    middle = rest.astype(BF16)
    low = (rest - middle.astype(F32)).astype(BF16)
    return high, middle, low


def iota(shape, dim):
    return lax.broadcasted_iota(jnp.int32, shape, dim)


def lane_onehot(idx, lanes):
    lane_of = idx & (lanes - 1)
    pieces = []
    for row in range(idx.shape[0]):
        hit = iota((lanes, idx.shape[1]), 0) == lane_of[row : row + 1, :]
        pieces.append(jnp.where(hit, F32(1.0), F32(0.0)).astype(BF16))
    return jnp.concatenate(pieces, axis=1)


def row_hit(idx, row, lanes, count):
    shift = lanes.bit_length() - 1
    row_of = lax.shift_right_logical(idx[row : row + 1, :], shift)
    return iota((count, idx.shape[1]), 0) == row_of


def scatter(flux, idx, lane_hot, count, lanes):
    parts = [part.astype(F32) for part in split3(flux)]
    columns = []
    for row in range(idx.shape[0]):
        hit = row_hit(idx, row, lanes, count)
        columns.append(
            jnp.concatenate(
                [jnp.where(hit, part[row : row + 1, :], F32(0.0)).astype(BF16) for part in parts],
                axis=0,
            )
        )
    spread = jnp.concatenate(columns, axis=1)
    out = lax.dot_general(
        spread, lane_hot, (((1,), (1,)), ((), ())), preferred_element_type=F32
    )
    return out[:count] + out[count : 2 * count] + out[2 * count :]


def gather(cells, idx, lane_hot, lanes):
    count = cells.shape[0]
    stacked = jnp.concatenate(split3(cells), axis=0)
    picked = lax.dot_general(
        stacked, lane_hot, (((1,), (0,)), ((), ())), preferred_element_type=F32
    )
    picked = picked[:count] + picked[count : 2 * count] + picked[2 * count :]
    slots = idx.shape[1]
    out = jnp.zeros(idx.shape, F32)
    for row in range(idx.shape[0]):
        part = jnp.where(
            row_hit(idx, row, lanes, count), picked[:, row * slots : (row + 1) * slots], F32(0.0)
        )
        total = jnp.sum(part, axis=0, keepdims=True)
        out = jnp.where(iota(idx.shape, 0) == row, total, out)
    return out


def well_update(rate, index, fm, seg, cell_p):
    slots = seg.shape[1]
    fp = pltpu.roll(fm, slots - 1, 1)
    seg_prev = pltpu.roll(seg, 1, 1)
    seg_next = pltpu.roll(seg, slots - 1, 1)
    seg_res = rate - (
        index * (seg - cell_p) + fm * (seg - seg_prev) + fp * (seg - seg_next)
    )
    return seg + F32(0.8) * seg_res / (index + fm + fp)


def y_shifted(block, edge, step):
    planes = []
    size = block.shape[1]
    for x in range(block.shape[0]):
        moved = pltpu.roll(block[x], (-step) % size, 0)
        at = size - 1 if step > 0 else 0
        planes.append(jnp.where(iota(moved.shape, 0) == at, edge[x : x + 1, :], moved))
    return planes


def z_shifted(plane, step):
    size = plane.shape[1]
    moved = pltpu.roll(plane, (-step) % size, 1)
    at = size - 1 if step > 0 else 0
    return jnp.where(iota(plane.shape, 1) == at, F32(0.0), moved)


def send_out(pos, odd, ring, vals, p, send_ref, face_ref, mate_ref, reach):
    width = p.shape[0]
    rows = vals.shape[0]
    send_ref[...] = jnp.zeros(send_ref.shape, F32)
    for d in range(1 - reach, reach):
        send_ref[lax.rem(pos + d + ring, ring), :rows, :] = vals
    send_ref[lax.rem(pos + 1, ring), rows:, :] = p[width - 1]
    send_ref[lax.rem(pos + ring - 1, ring), rows:, :] = p[0]
    for x in range(width):
        low, high = p[x][:1, :], p[x][-1:, :]
        face_ref[x : x + 1, :] = jnp.where(odd, high, low)
        mate_ref[x : x + 1, :] = jnp.where(odd, low, high)


def pack_kernel(pos_ref, tx_ref, ty_ref, host_ref, index_ref, cond_ref, rate_ref, send_ref, yhi_ref, *, reach):
    pos = pos_ref[0]
    ring = send_ref.shape[0]
    width = tx_ref.shape[0]
    pack = jnp.concatenate(
        [host_ref[0].astype(F32), index_ref[0], cond_ref[0], rate_ref[0]], axis=0
    )
    rows = pack.shape[0]
    send_ref[...] = jnp.zeros(send_ref.shape, F32)
    for d in range(reach):
        send_ref[lax.rem(pos + d, ring), :rows, :] = pack
    send_ref[lax.rem(pos + 1, ring), rows:, :] = tx_ref[width - 1]
    for x in range(width):
        yhi_ref[x : x + 1, :] = ty_ref[x, ty_ref.shape[1] - 1 :, :]


def first_kernel(
    pos_ref, rhs_ref, acc_ref, tx_ref, ty_ref, tz_ref, recv_ref, wy_ref, held_ref,
    p_ref, gain_ref, wx_ref, seg_ref, well_ref, send_ref, face_ref, mate_ref, *, reach, wells,
):
    pos = pos_ref[0]
    odd = pos_ref[1] == 1
    ring = recv_ref.shape[0]
    width, depth, lanes = rhs_ref.shape
    rows = reach * wells
    slots = lanes
    groups = []
    for array in range(4):
        whole = jnp.zeros((rows, slots), F32)
        for q in range(reach):
            piece = recv_ref[lax.rem(pos + ring - q, ring), :rows, :]
            moved = pltpu.roll(piece, (wells * (q - array)) % rows, 0) if q != array else piece
            whole = jnp.where(iota((rows, slots), 0) // wells == q, moved, whole)
        groups.append(whole)
    host, index, cond, rate = groups
    fm = jnp.where(iota((rows, slots), 1) > 0, cond, F32(0.0))
    well_ref[0], well_ref[1], well_ref[2], well_ref[3] = host, index, fm, rate
    zero = jnp.zeros((rows, slots), F32)
    seg = well_update(rate, index, fm, zero, zero)
    seg_ref[...] = seg
    flux = F32(0.0) - index * seg
    idx = held_ref[...].reshape(rows, slots)
    own = (iota((rows, slots), 0) // wells).astype(F32)
    flux = jnp.where(host == own, flux, F32(0.0))
    hot = lane_onehot(idx, lanes)
    count = width * depth
    well_term = scatter(flux, idx, hot, count, lanes).reshape(width, depth, lanes)
    west = jnp.where(pos == 0, F32(0.0), recv_ref[lax.rem(pos + ring - 1, ring), rows:, :])
    wx_ref[...] = west
    wy = y_shifted(ty_ref[...], wy_ref[...], -1)
    planes = []
    for x in range(width):
        tz = tz_ref[x]
        diag = acc_ref[x] + tx_ref[x] + (west if x == 0 else tx_ref[x - 1])
        diag = diag + ty_ref[x] + wy[x] + tz + z_shifted(tz, -1)
        gain = F32(0.7) / diag
        gain_ref[x] = gain
        planes.append(gain * (rhs_ref[x] - well_term[x]))
    for x in range(width):
        p_ref[x] = planes[x]
    cells = jnp.concatenate(planes, axis=0)
    vals = gather(cells, idx, hot, lanes)
    send_out(pos, odd, ring, vals, planes_array(planes), send_ref, face_ref, mate_ref, reach)


class planes_array:
    def __init__(self, planes):
        self.planes = planes
        self.shape = (len(planes), *planes[0].shape)

    def __getitem__(self, x):
        return self.planes[x]


def sweep_kernel(
    pos_ref, p_in, rhs_ref, tx_ref, ty_ref, tz_ref, gain_ref, wx_ref, wy_ref, recv_ref, face_in, mate_in,
    seg_in, well_ref, held_ref, p_ref, seg_ref, *rest, reach, wells, last,
):
    pos = pos_ref[0]
    odd = pos_ref[1] == 1
    ring = recv_ref.shape[0]
    width, depth, lanes = rhs_ref.shape
    rows = reach * wells
    slots = lanes
    host, index, fm, rate = well_ref[0], well_ref[1], well_ref[2], well_ref[3]
    own_row = iota((rows, slots), 0) // wells
    cell_p = jnp.zeros((rows, slots), F32)
    for d in range(1 - reach, reach):
        piece = recv_ref[lax.rem(pos + d + ring, ring), :rows, :]
        moved = pltpu.roll(piece, (-wells * d) % rows, 0) if d else piece
        cell_p = jnp.where(host == (own_row + d).astype(F32), moved, cell_p)
    seg = well_update(rate, index, fm, seg_in[...], cell_p)
    if last:
        seg_ref[0] = seg[:wells]
    else:
        seg_ref[...] = seg
    flux = index * (cell_p - seg)
    flux = jnp.where(host == own_row.astype(F32), flux, F32(0.0))
    idx = held_ref[...].reshape(rows, slots)
    hot = lane_onehot(idx, lanes)
    count = width * depth
    well_term = scatter(flux, idx, hot, count, lanes).reshape(width, depth, lanes)
    west = jnp.where(pos == 0, F32(0.0), recv_ref[lax.rem(pos + ring - 1, ring), rows:, :])
    east = jnp.where(pos == ring - 1, F32(0.0), recv_ref[lax.rem(pos + 1, ring), rows:, :])
    block = p_in[...]
    wy = y_shifted(ty_ref[...], wy_ref[...], -1)
    face, mate = face_in[...], mate_in[...]
    south = y_shifted(block, jnp.where(odd, mate, face), -1)
    north = y_shifted(block, jnp.where(odd, face, mate), 1)
    planes = []
    for x in range(width):
        tz = tz_ref[x]
        total = rhs_ref[x] - well_term[x]
        total = total + tx_ref[x] * (east if x == width - 1 else block[x + 1])
        total = total + (wx_ref[...] * west if x == 0 else tx_ref[x - 1] * block[x - 1])
        total = total + ty_ref[x] * north[x] + wy[x] * south[x]
        total = total + tz * z_shifted(block[x], 1) + z_shifted(tz, -1) * z_shifted(block[x], -1)
        planes.append(F32(0.3) * block[x] + gain_ref[x] * total)
    for x in range(width):
        p_ref[x] = planes[x]
    if not last:
        send_ref, face_ref, mate_ref = rest
        vals = gather(jnp.concatenate(planes, axis=0), idx, hot, lanes)
        send_out(pos, odd, ring, vals, planes_array(planes), send_ref, face_ref, mate_ref, reach)


def shards(
    rhs_field,
    accumulation,
    trans_x,
    trans_y,
    trans_z,
    held_cells,
    perf_host,
    well_index,
    seg_cond,
    seg_rate,
):
    width, depth, layers = rhs_field.shape
    reach = held_cells.shape[0]
    wells = well_index.shape[1]
    slots = well_index.shape[2]
    rows = reach * wells
    ring = lax.axis_size("gx")
    county = lax.axis_size("gy")
    up = [(j, j + 1) for j in range(county - 1)]
    facing = [(j, j + 1) for j in range(1, county - 1, 2)]
    facing += [(target, source) for source, target in facing]
    mates = [(j, j ^ 1) for j in range(county)]
    pos = jnp.stack([lax.axis_index("gx"), lax.axis_index("gy") & 1]).astype(jnp.int32)

    def shape(*dims):
        return pltpu.VMEM(dims, F32)

    def result(*dims):
        return jax.ShapeDtypeStruct(dims, F32)

    def near(value):
        return pltpu.with_memory_space_constraint(value, pltpu.VMEM)

    smem = pl.BlockSpec(memory_space=pltpu.SMEM)
    vmem = pl.BlockSpec(memory_space=pltpu.VMEM)

    def call(body, outs, *args, **static):
        return pl.pallas_call(
            lambda *refs: body(*refs, **static),
            out_shape=outs,
            in_specs=[smem] + [vmem] * (len(args) - 1),
            out_specs=[vmem] * len(outs),
        )(args[0], *map(near, args[1:]))

    message = shape(ring, rows + depth, slots)
    edge = shape(width, layers)
    block = shape(width, depth, layers)

    def exchanged(send):
        return lax.all_to_all(send, "gx", 0, 0, tiled=True)

    send, yhi = call(
        pack_kernel, [message, edge], pos, trans_x, trans_y, perf_host, well_index, seg_cond, seg_rate,
        reach=reach,
    )
    wy = lax.ppermute(yhi, "gy", up)
    recv = exchanged(send)
    p, gain, wx, seg, well, send, face, mate = call(
        first_kernel,
        [block, block, shape(depth, layers), shape(rows, slots), shape(4, rows, slots), message, edge, edge],
        pos, rhs_field, accumulation, trans_x, trans_y, trans_z, recv, wy, held_cells,
        reach=reach, wells=wells,
    )
    for sweep in range(1, SWEEPS):
        last = sweep == SWEEPS - 1
        face_in = lax.ppermute(face, "gy", facing)
        mate_in = lax.ppermute(mate, "gy", mates)
        recv = exchanged(send)
        outs = [result(width, depth, layers), result(1, wells, slots)] if last else [block, shape(rows, slots)]
        if not last:
            outs += [message, edge, edge]
        got = call(
            sweep_kernel, outs, pos, p, rhs_field, trans_x, trans_y, trans_z, gain, wx, wy, recv, face_in, mate_in,
            seg, well, held_cells, reach=reach, wells=wells, last=last,
        )
        p, seg = got[:2]
        if not last:
            send, face, mate = got[2:]
    return (p, seg)


def solution(mesh):
    return jax.shard_map(
        shards,
        mesh=mesh,
        in_specs=(
            P("gx", "gy", None),
            P("gx", "gy", None),
            P("gx", "gy", None),
            P("gx", "gy", None),
            P("gx", "gy", None),
            P(None, "gx", "gy", None),
            P("gx", "gy", None),
            P("gx", "gy", None),
            P("gx", "gy", None),
            P("gx", "gy", None),
        ),
        out_specs=(P("gx", "gy", None), P("gx", "gy", None)),
        check_vma=False,
    )
```

```python
import jax
import jax.numpy as jnp
from jax import lax
from jax.experimental import pallas as pl
from jax.experimental.pallas import tpu as pltpu
from jax.sharding import PartitionSpec as P

SWEEPS = 6
F32 = jnp.float32
BF16 = jnp.bfloat16


def split3(value):
    high = value.astype(BF16)
    rest = value - high.astype(F32)
    middle = rest.astype(BF16)
    low = (rest - middle.astype(F32)).astype(BF16)
    return high, middle, low


def iota(shape, dim):
    return lax.broadcasted_iota(jnp.int32, shape, dim)


def lane_onehot(idx, lanes):
    lane_of = idx & (lanes - 1)
    pieces = []
    for row in range(idx.shape[0]):
        hit = iota((lanes, idx.shape[1]), 0) == lane_of[row : row + 1, :]
        pieces.append(jnp.where(hit, F32(1.0), F32(0.0)).astype(BF16))
    return jnp.concatenate(pieces, axis=1)


def row_hit(idx, row, lanes, count):
    shift = lanes.bit_length() - 1
    row_of = lax.shift_right_logical(idx[row : row + 1, :], shift)
    return iota((count, idx.shape[1]), 0) == row_of


def scatter(flux, idx, lane_hot, count, lanes):
    parts = [part.astype(F32) for part in split3(flux)]
    columns = []
    for row in range(idx.shape[0]):
        hit = row_hit(idx, row, lanes, count)
        columns.append(
            jnp.concatenate(
                [jnp.where(hit, part[row : row + 1, :], F32(0.0)).astype(BF16) for part in parts],
                axis=0,
            )
        )
    spread = jnp.concatenate(columns, axis=1)
    out = lax.dot_general(
        spread, lane_hot, (((1,), (1,)), ((), ())), preferred_element_type=F32
    )
    return out[:count] + out[count : 2 * count] + out[2 * count :]


def gather(cells, idx, lane_hot, lanes):
    count = cells.shape[0]
    stacked = jnp.concatenate(split3(cells), axis=0)
    picked = lax.dot_general(
        stacked, lane_hot, (((1,), (0,)), ((), ())), preferred_element_type=F32
    )
    picked = picked[:count] + picked[count : 2 * count] + picked[2 * count :]
    slots = idx.shape[1]
    out = jnp.zeros(idx.shape, F32)
    for row in range(idx.shape[0]):
        part = jnp.where(
            row_hit(idx, row, lanes, count), picked[:, row * slots : (row + 1) * slots], F32(0.0)
        )
        total = jnp.sum(part, axis=0, keepdims=True)
        out = jnp.where(iota(idx.shape, 0) == row, total, out)
    return out


def well_update(rate, index, fm, seg, cell_p):
    slots = seg.shape[1]
    fp = pltpu.roll(fm, slots - 1, 1)
    seg_prev = pltpu.roll(seg, 1, 1)
    seg_next = pltpu.roll(seg, slots - 1, 1)
    seg_res = rate - (
        index * (seg - cell_p) + fm * (seg - seg_prev) + fp * (seg - seg_next)
    )
    return seg + F32(0.8) * seg_res / (index + fm + fp)


def y_shifted(block, edge, step):
    planes = []
    size = block.shape[1]
    for x in range(block.shape[0]):
        moved = pltpu.roll(block[x], (-step) % size, 0)
        at = size - 1 if step > 0 else 0
        planes.append(jnp.where(iota(moved.shape, 0) == at, edge[x : x + 1, :], moved))
    return planes


def z_shifted(plane, step):
    size = plane.shape[1]
    moved = pltpu.roll(plane, (-step) % size, 1)
    at = size - 1 if step > 0 else 0
    return jnp.where(iota(plane.shape, 1) == at, F32(0.0), moved)


def send_out(pos, odd, ring, vals, p, send_ref, face_ref, mate_ref, reach):
    width = p.shape[0]
    rows = vals.shape[0]
    send_ref[...] = jnp.zeros(send_ref.shape, F32)
    for d in range(1 - reach, reach):
        send_ref[lax.rem(pos + d + ring, ring), :rows, :] = vals
    send_ref[lax.rem(pos + 1, ring), rows:, :] = p[width - 1]
    send_ref[lax.rem(pos + ring - 1, ring), rows:, :] = p[0]
    for x in range(width):
        low, high = p[x][:1, :], p[x][-1:, :]
        face_ref[x : x + 1, :] = jnp.where(odd, high, low)
        mate_ref[x : x + 1, :] = jnp.where(odd, low, high)


def pack_kernel(tx_ref, ty_ref, host_ref, index_ref, cond_ref, rate_ref, send_ref, yhi_ref, *, reach):
    pos = lax.axis_index("gx")
    ring = send_ref.shape[0]
    width = tx_ref.shape[0]
    pack = jnp.concatenate(
        [host_ref[0].astype(F32), index_ref[0], cond_ref[0], rate_ref[0]], axis=0
    )
    rows = pack.shape[0]
    send_ref[...] = jnp.zeros(send_ref.shape, F32)
    for d in range(reach):
        send_ref[lax.rem(pos + d, ring), :rows, :] = pack
    send_ref[lax.rem(pos + 1, ring), rows:, :] = tx_ref[width - 1]
    for x in range(width):
        yhi_ref[x : x + 1, :] = ty_ref[x, ty_ref.shape[1] - 1 :, :]


def first_kernel(
    rhs_ref, acc_ref, tx_ref, ty_ref, tz_ref, recv_ref, wy_ref, held_ref,
    p_ref, gain_ref, wx_ref, seg_ref, well_ref, send_ref, face_ref, mate_ref, *, reach, wells,
):
    pos = lax.axis_index("gx")
    odd = (lax.axis_index("gy") & 1) == 1
    ring = recv_ref.shape[0]
    width, depth, lanes = rhs_ref.shape
    rows = reach * wells
    slots = lanes
    groups = []
    for array in range(4):
        whole = jnp.zeros((rows, slots), F32)
        for q in range(reach):
            piece = recv_ref[lax.rem(pos + ring - q, ring), :rows, :]
            moved = pltpu.roll(piece, (wells * (q - array)) % rows, 0) if q != array else piece
            whole = jnp.where(iota((rows, slots), 0) // wells == q, moved, whole)
        groups.append(whole)
    host, index, cond, rate = groups
    fm = jnp.where(iota((rows, slots), 1) > 0, cond, F32(0.0))
    well_ref[0], well_ref[1], well_ref[2], well_ref[3] = host, index, fm, rate
    zero = jnp.zeros((rows, slots), F32)
    seg = well_update(rate, index, fm, zero, zero)
    seg_ref[...] = seg
    flux = F32(0.0) - index * seg
    idx = held_ref[...].reshape(rows, slots)
    own = (iota((rows, slots), 0) // wells).astype(F32)
    flux = jnp.where(host == own, flux, F32(0.0))
    hot = lane_onehot(idx, lanes)
    count = width * depth
    well_term = scatter(flux, idx, hot, count, lanes).reshape(width, depth, lanes)
    west = jnp.where(pos == 0, F32(0.0), recv_ref[lax.rem(pos + ring - 1, ring), rows:, :])
    wx_ref[...] = west
    wy = y_shifted(ty_ref[...], wy_ref[...], -1)
    planes = []
    for x in range(width):
        tz = tz_ref[x]
        diag = acc_ref[x] + tx_ref[x] + (west if x == 0 else tx_ref[x - 1])
        diag = diag + ty_ref[x] + wy[x] + tz + z_shifted(tz, -1)
        gain = F32(0.7) / diag
        gain_ref[x] = gain
        planes.append(gain * (rhs_ref[x] - well_term[x]))
    for x in range(width):
        p_ref[x] = planes[x]
    cells = jnp.concatenate(planes, axis=0)
    vals = gather(cells, idx, hot, lanes)
    send_out(pos, odd, ring, vals, planes_array(planes), send_ref, face_ref, mate_ref, reach)


class planes_array:
    def __init__(self, planes):
        self.planes = planes
        self.shape = (len(planes), *planes[0].shape)

    def __getitem__(self, x):
        return self.planes[x]


def sweep_kernel(
    p_in, rhs_ref, tx_ref, ty_ref, tz_ref, gain_ref, wx_ref, wy_ref, recv_ref, face_in, mate_in,
    seg_in, well_ref, held_ref, p_ref, seg_ref, *rest, reach, wells, last,
):
    pos = lax.axis_index("gx")
    odd = (lax.axis_index("gy") & 1) == 1
    ring = recv_ref.shape[0]
    width, depth, lanes = rhs_ref.shape
    rows = reach * wells
    slots = lanes
    host, index, fm, rate = well_ref[0], well_ref[1], well_ref[2], well_ref[3]
    own_row = iota((rows, slots), 0) // wells
    cell_p = jnp.zeros((rows, slots), F32)
    for d in range(1 - reach, reach):
        piece = recv_ref[lax.rem(pos + d + ring, ring), :rows, :]
        moved = pltpu.roll(piece, (-wells * d) % rows, 0) if d else piece
        cell_p = jnp.where(host == (own_row + d).astype(F32), moved, cell_p)
    seg = well_update(rate, index, fm, seg_in[...], cell_p)
    if last:
        seg_ref[0] = seg[:wells]
    else:
        seg_ref[...] = seg
    flux = index * (cell_p - seg)
    flux = jnp.where(host == own_row.astype(F32), flux, F32(0.0))
    idx = held_ref[...].reshape(rows, slots)
    hot = lane_onehot(idx, lanes)
    count = width * depth
    well_term = scatter(flux, idx, hot, count, lanes).reshape(width, depth, lanes)
    west = jnp.where(pos == 0, F32(0.0), recv_ref[lax.rem(pos + ring - 1, ring), rows:, :])
    east = jnp.where(pos == ring - 1, F32(0.0), recv_ref[lax.rem(pos + 1, ring), rows:, :])
    block = p_in[...]
    wy = y_shifted(ty_ref[...], wy_ref[...], -1)
    face, mate = face_in[...], mate_in[...]
    south = y_shifted(block, jnp.where(odd, mate, face), -1)
    north = y_shifted(block, jnp.where(odd, face, mate), 1)
    planes = []
    for x in range(width):
        tz = tz_ref[x]
        total = rhs_ref[x] - well_term[x]
        total = total + tx_ref[x] * (east if x == width - 1 else block[x + 1])
        total = total + (wx_ref[...] * west if x == 0 else tx_ref[x - 1] * block[x - 1])
        total = total + ty_ref[x] * north[x] + wy[x] * south[x]
        total = total + tz * z_shifted(block[x], 1) + z_shifted(tz, -1) * z_shifted(block[x], -1)
        planes.append(F32(0.3) * block[x] + gain_ref[x] * total)
    for x in range(width):
        p_ref[x] = planes[x]
    if not last:
        send_ref, face_ref, mate_ref = rest
        vals = gather(jnp.concatenate(planes, axis=0), idx, hot, lanes)
        send_out(pos, odd, ring, vals, planes_array(planes), send_ref, face_ref, mate_ref, reach)


def shards(
    rhs_field,
    accumulation,
    trans_x,
    trans_y,
    trans_z,
    held_cells,
    perf_host,
    well_index,
    seg_cond,
    seg_rate,
):
    width, depth, layers = rhs_field.shape
    reach = held_cells.shape[0]
    wells = well_index.shape[1]
    slots = well_index.shape[2]
    rows = reach * wells
    ring = lax.axis_size("gx")
    county = lax.axis_size("gy")
    up = [(j, j + 1) for j in range(county - 1)]
    facing = [(j, j + 1) for j in range(1, county - 1, 2)]
    facing += [(target, source) for source, target in facing]
    mates = [(j, j ^ 1) for j in range(county)]

    def shape(*dims):
        return pltpu.VMEM(dims, F32)

    def result(*dims):
        return jax.ShapeDtypeStruct(dims, F32)

    def near(value):
        return pltpu.with_memory_space_constraint(value, pltpu.VMEM)

    vmem = pl.BlockSpec(memory_space=pltpu.VMEM)

    def call(body, outs, *args, placed=near, **static):
        return pl.pallas_call(
            lambda *refs: body(*refs, **static),
            out_shape=outs,
            in_specs=[vmem] * len(args),
            out_specs=[vmem] * len(outs),
        )(*map(placed, args))

    message = shape(ring, rows + depth, slots)
    edge = shape(width, layers)
    block = shape(width, depth, layers)

    def exchanged(send):
        return lax.all_to_all(send, "gx", 0, 0, tiled=True)

    send, yhi = call(
        pack_kernel, [message, edge], trans_x, trans_y, perf_host, well_index, seg_cond, seg_rate,
        placed=lambda value: value, reach=reach,
    )
    wy = lax.ppermute(yhi, "gy", up)
    recv = exchanged(send)
    p, gain, wx, seg, well, send, face, mate = call(
        first_kernel,
        [block, block, shape(depth, layers), shape(rows, slots), shape(4, rows, slots), message, edge, edge],
        rhs_field, accumulation, trans_x, trans_y, trans_z, recv, wy, held_cells,
        reach=reach, wells=wells,
    )
    for sweep in range(1, SWEEPS):
        last = sweep == SWEEPS - 1
        face_in = lax.ppermute(face, "gy", facing)
        mate_in = lax.ppermute(mate, "gy", mates)
        recv = exchanged(send)
        outs = [result(width, depth, layers), result(1, wells, slots)] if last else [block, shape(rows, slots)]
        if not last:
            outs += [message, edge, edge]
        got = call(
            sweep_kernel, outs, p, rhs_field, trans_x, trans_y, trans_z, gain, wx, wy, recv, face_in, mate_in,
            seg, well, held_cells, reach=reach, wells=wells, last=last,
        )
        p, seg = got[:2]
        if not last:
            send, face, mate = got[2:]
    return (p, seg)


def solution(mesh):
    return jax.shard_map(
        shards,
        mesh=mesh,
        in_specs=(
            P("gx", "gy", None),
            P("gx", "gy", None),
            P("gx", "gy", None),
            P("gx", "gy", None),
            P("gx", "gy", None),
            P(None, "gx", "gy", None),
            P("gx", "gy", None),
            P("gx", "gy", None),
            P("gx", "gy", None),
            P("gx", "gy", None),
        ),
        out_specs=(P("gx", "gy", None), P("gx", "gy", None)),
        check_vma=False,
    )
```

```python
import jax
import jax.numpy as jnp
from jax import lax
from jax.experimental import pallas as pl
from jax.experimental.pallas import tpu as pltpu
from jax.sharding import PartitionSpec as P

SWEEPS = 6
F32 = jnp.float32
BF16 = jnp.bfloat16


def split3(value):
    high = value.astype(BF16)
    rest = value - high.astype(F32)
    middle = rest.astype(BF16)
    low = (rest - middle.astype(F32)).astype(BF16)
    return high, middle, low


def iota(shape, dim):
    return lax.broadcasted_iota(jnp.int32, shape, dim)


def lane_onehot(idx, lanes):
    lane_of = idx & (lanes - 1)
    pieces = []
    for row in range(idx.shape[0]):
        hit = iota((lanes, idx.shape[1]), 0) == lane_of[row : row + 1, :]
        pieces.append(jnp.where(hit, F32(1.0), F32(0.0)).astype(BF16))
    return jnp.concatenate(pieces, axis=1)


def row_hit(idx, row, lanes, count):
    shift = lanes.bit_length() - 1
    row_of = lax.shift_right_logical(idx[row : row + 1, :], shift)
    return iota((count, idx.shape[1]), 0) == row_of


def scatter(flux, idx, lane_hot, count, lanes):
    parts = [part.astype(F32) for part in split3(flux)]
    columns = []
    for row in range(idx.shape[0]):
        hit = row_hit(idx, row, lanes, count)
        columns.append(
            jnp.concatenate(
                [jnp.where(hit, part[row : row + 1, :], F32(0.0)).astype(BF16) for part in parts],
                axis=0,
            )
        )
    spread = jnp.concatenate(columns, axis=1)
    out = lax.dot_general(
        spread, lane_hot, (((1,), (1,)), ((), ())), preferred_element_type=F32
    )
    return out[:count] + out[count : 2 * count] + out[2 * count :]


def gather(cells, idx, lane_hot, lanes):
    count = cells.shape[0]
    stacked = jnp.concatenate(split3(cells), axis=0)
    picked = lax.dot_general(
        stacked, lane_hot, (((1,), (0,)), ((), ())), preferred_element_type=F32
    )
    picked = picked[:count] + picked[count : 2 * count] + picked[2 * count :]
    slots = idx.shape[1]
    out = jnp.zeros(idx.shape, F32)
    for row in range(idx.shape[0]):
        part = jnp.where(
            row_hit(idx, row, lanes, count), picked[:, row * slots : (row + 1) * slots], F32(0.0)
        )
        total = jnp.sum(part, axis=0, keepdims=True)
        out = jnp.where(iota(idx.shape, 0) == row, total, out)
    return out


def well_update(rate, index, fm, seg, cell_p):
    slots = seg.shape[1]
    fp = pltpu.roll(fm, slots - 1, 1)
    seg_prev = pltpu.roll(seg, 1, 1)
    seg_next = pltpu.roll(seg, slots - 1, 1)
    seg_res = rate - (
        index * (seg - cell_p) + fm * (seg - seg_prev) + fp * (seg - seg_next)
    )
    return seg + F32(0.8) * seg_res / (index + fm + fp)


UNIT = 4
PARTS = 48


def z_shifted(plane, step):
    size = plane.shape[1]
    moved = pltpu.roll(plane, (-step) % size, 1)
    at = size - 1 if step > 0 else 0
    return jnp.where(iota(plane.shape, 1) == at, F32(0.0), moved)


def y_moved(plane, edge, step):
    size = plane.shape[0]
    at = size - 1 if step > 0 else 0
    return jnp.where(iota(plane.shape, 0) == at, edge, pltpu.roll(plane, (-step) % size, 0))


def places():
    unit = lax.axis_index("gx") // UNIT
    odd = unit & 1
    half = 4 * PARTS + 8 * UNIT
    return unit, odd * 2 * PARTS, odd * half + 2 * PARTS, (1 - odd) * half


def rows_at(recv_ref, start, count=8):
    return recv_ref[pl.ds(pl.multiple_of(start, 8), count), :]


def lifted(piece, shift):
    tall = jnp.concatenate([piece, jnp.zeros_like(piece)], axis=0)
    shift = shift % tall.shape[0]
    return pltpu.roll(tall, shift, 0) if shift else tall


def window(rows, y, block):
    start = 16 * y + 6 - 2 * block
    moved = pltpu.roll(rows, (-start) % rows.shape[0], 0) if start else rows
    return moved[:8]


def spread_wells(flux, host, held_ref, term_ref):
    hots = []
    for y in range(2):
        for block in range(UNIT):
            near_host = window(host, y, block)
            part = window(flux, y, block)
            part = jnp.where(near_host == (iota(part.shape, 0) // 2).astype(F32), part, F32(0.0))
            idx = held_ref[2 * block + y]
            hot = lane_onehot(idx, 128)
            hots.append(hot)
            term = scatter(part, idx, hot, 64, 128)
            term_ref[pl.ds(32 * y + 8 * block, 8)] = term.reshape(8, 8, 128)
    return hots


def send_out(p_ref, held_ref, hots, send_ref, face_ref):
    for y in range(2):
        for block in range(UNIT):
            cells = p_ref[pl.ds(32 * y + 8 * block, 8)].reshape(64, 128)
            vals = gather(cells, held_ref[2 * block + y], hots[UNIT * y + block], 128)
            send_ref[pl.ds(PARTS * y + 8 * block, 8), :] = vals
        send_ref[pl.ds(PARTS * y + 32, 8), :] = p_ref[32 * y]
        send_ref[pl.ds(PARTS * y + 40, 8), :] = p_ref[32 * y + 31]
    upper = (lax.axis_index("gy") & 1) == 1
    for x in range(32):
        face_ref[x : x + 1, :] = jnp.where(upper, p_ref[32 + x, 7:8, :], p_ref[x, 0:1, :])


def field(fields_ref, which, y, x):
    return fields_ref[2 * (x // 8) + y, pl.ds(64 * which + 8 * (x % 8), 8), :]


def pack_kernel(
    rhs_ref, acc_ref, tx_ref, ty_ref, tz_ref, held_ref, host_ref, index_ref, cond_ref, rate_ref, small_ref, large_ref
):
    members = large_ref.shape[0]
    pack = jnp.concatenate(
        [host_ref[0].astype(F32), index_ref[0], cond_ref[0], rate_ref[0]], axis=0
    )
    edge = jnp.concatenate([ty_ref[x, 7:8, :] for x in range(8)], axis=0)
    for m in range(members):
        small_ref[m, 0:8, :] = pack
        small_ref[m, 8:16, :] = tx_ref[7]
        small_ref[m, 16:24, :] = edge
    for which, ref in enumerate((rhs_ref, acc_ref, tx_ref, ty_ref, tz_ref)):
        whole = ref[...].reshape(64, 128)
        for m in range(members):
            large_ref[m, 64 * which : 64 * which + 64, :] = whole
    held = held_ref[...].reshape(8, 128).astype(F32)
    for m in range(members):
        large_ref[m, 320:328, :] = held


def share_kernel(small_ref, send_ref, face_ref):
    for y in range(2):
        for block in range(UNIT):
            send_ref[pl.ds(PARTS * y + 8 * block, 8), :] = small_ref[2 * block + y, 0:8, :]
        send_ref[pl.ds(PARTS * y + 32, 8), :] = jnp.zeros((8, 128), F32)
        send_ref[pl.ds(PARTS * y + 40, 8), :] = small_ref[2 * (UNIT - 1) + y, 8:16, :]
    for block in range(UNIT):
        face_ref[pl.ds(8 * block, 8), :] = small_ref[2 * block + 1, 16:24, :]


def first_kernel(
    fields_ref, recv_ref, p_ref, gain_ref, wx_ref, wy_ref, seg_ref, well_ref, held_ref, send_ref, face_ref, term_ref
):
    unit, here, after, before = places()
    own = iota((16, 128), 0) // 2
    groups = []
    for array in range(4):
        halves = []
        for y in range(2):
            whole = jnp.zeros((16, 128), F32)
            for owner in range(-UNIT, UNIT):
                base = here + 8 * owner if owner >= 0 else before + 8 * (owner + UNIT)
                place = UNIT - 1 - owner
                moved = lifted(rows_at(recv_ref, base + PARTS * y), 2 * place - 2 * array)
                whole = jnp.where(own == place, moved, whole)
            halves.append(whole)
        groups.append(jnp.concatenate(halves, axis=0))
    host, index, cond, rate = groups
    fm = jnp.where(iota(cond.shape, 1) > 0, cond, F32(0.0))
    well_ref[0], well_ref[1], well_ref[2], well_ref[3] = host, index, fm, rate
    zero = jnp.zeros(cond.shape, F32)
    seg = well_update(rate, index, fm, zero, zero)
    seg_ref[...] = seg
    for m in range(2 * UNIT):
        held_ref[m] = fields_ref[m, 320:328, :].astype(jnp.int32)
    hots = spread_wells(F32(0.0) - index * seg, host, held_ref, term_ref)
    wy_ref[...] = recv_ref[4 * PARTS : 4 * PARTS + 32, :]
    for y in range(2):
        west = rows_at(recv_ref, before + PARTS * y + 40)
        west = jnp.where(unit == 0, F32(0.0), west)
        wx_ref[y] = west
        for x in range(32):
            tx, ty, tz = (field(fields_ref, which, y, x) for which in (2, 3, 4))
            edge = field(fields_ref, 3, 0, x)[7:8, :] if y else wy_ref[x : x + 1, :]
            diag = field(fields_ref, 1, y, x) + tx + (field(fields_ref, 2, y, x - 1) if x else west)
            diag = diag + ty + y_moved(ty, edge, -1) + tz + z_shifted(tz, -1)
            gain = F32(0.7) / diag
            gain_ref[32 * y + x] = gain
            p_ref[32 * y + x] = gain * (field(fields_ref, 0, y, x) - term_ref[32 * y + x])
    send_out(p_ref, held_ref, hots, send_ref, face_ref)


def sweep_kernel(
    p_in, fields_ref, gain_ref, wx_ref, wy_ref, recv_ref, seg_in, well_ref, held_ref, *rest, last
):
    if last:
        out_ref, seg_out, p_ref, term_ref = rest
    else:
        p_ref, seg_ref, send_ref, face_ref, term_ref = rest
    unit, here, after, before = places()
    units = lax.axis_size("gx") // UNIT
    host, index, fm, rate = well_ref[0], well_ref[1], well_ref[2], well_ref[3]
    own = iota((16, 128), 0) // 2
    halves = []
    for y in range(2):
        cell = jnp.zeros((16, 128), F32)
        near_host = host[16 * y : 16 * y + 16]
        for block in range(1 - UNIT, 2 * UNIT - 1):
            base = here if 0 <= block < UNIT else after if block > 0 else before
            vals = rows_at(recv_ref, base + PARTS * y + 8 * (block % UNIT))
            hit = near_host == (own + block - 3).astype(F32)
            cell = jnp.where(hit, lifted(vals, 6 - 2 * block), cell)
        halves.append(cell)
    cell_p = jnp.concatenate(halves, axis=0)
    seg = well_update(rate, index, fm, seg_in[...], cell_p)
    hots = spread_wells(index * (cell_p - seg), host, held_ref, term_ref)
    half = 4 * PARTS + 32
    for y in range(2):
        west = rows_at(recv_ref, before + PARTS * y + 40)
        west = jnp.where(unit == 0, F32(0.0), west)
        east = rows_at(recv_ref, after + PARTS * y + 32)
        east = jnp.where(unit == units - 1, F32(0.0), east)
        for x in range(32):
            block = p_in[32 * y + x]
            tx, ty, tz = (field(fields_ref, which, y, x) for which in (2, 3, 4))
            if y:
                south, north = p_in[x, 7:8, :], recv_ref[half + 4 * PARTS + x : half + 4 * PARTS + x + 1, :]
                edge = field(fields_ref, 3, 0, x)[7:8, :]
            else:
                south, north = recv_ref[4 * PARTS + x : 4 * PARTS + x + 1, :], p_in[32 + x, 0:1, :]
                edge = wy_ref[x : x + 1, :]
            total = field(fields_ref, 0, y, x) - term_ref[32 * y + x]
            total = total + tx * (p_in[32 * y + x + 1] if x < 31 else east)
            if x:
                total = total + field(fields_ref, 2, y, x - 1) * p_in[32 * y + x - 1]
            else:
                total = total + wx_ref[y] * west
            total = total + ty * y_moved(block, north, 1) + y_moved(ty, edge, -1) * y_moved(block, south, -1)
            total = total + tz * z_shifted(block, 1) + z_shifted(tz, -1) * z_shifted(block, -1)
            p_ref[32 * y + x] = F32(0.3) * block + gain_ref[32 * y + x] * total
    if last:
        at = lax.axis_index("gx") % UNIT
        core = lax.axis_index("gy") & 1
        out_ref[...] = p_ref[pl.ds(32 * core + 8 * at, 8)]
        mine = seg[6:8]
        for y in range(2):
            for owner in range(UNIT):
                start = 16 * y + 2 * (UNIT - 1 - owner)
                mine = jnp.where((at == owner) & (core == y), seg[start : start + 2], mine)
        seg_out[0] = mine
    else:
        seg_ref[...] = seg
        send_out(p_ref, held_ref, hots, send_ref, face_ref)


def shards(
    rhs_field,
    accumulation,
    trans_x,
    trans_y,
    trans_z,
    held_cells,
    perf_host,
    well_index,
    seg_cond,
    seg_rate,
):
    ring = lax.axis_size("gx")
    county = lax.axis_size("gy")
    units = ring // UNIT
    facing = [(j, j + 1) for j in range(1, county - 1, 2)]
    facing += [(target, source) for source, target in facing]
    mates = [[j, j + 1] for j in range(0, county, 2)]
    chips = [
        [(UNIT * unit + x) * county + j + core for x in range(UNIT) for core in range(2)]
        for unit in range(units)
        for j in range(0, county, 2)
    ]
    columns = [
        [(((low + step + j % 2) % units) * UNIT + x) * county + j for step in range(2)]
        for j in range(county)
        for low in range(0, units, 2)
        for x in range(UNIT)
    ]

    def shape(*dims):
        return pltpu.VMEM(dims, F32)

    def result(*dims):
        return jax.ShapeDtypeStruct(dims, F32)

    def near(value):
        return pltpu.with_memory_space_constraint(value, pltpu.VMEM)

    vmem = pl.BlockSpec(memory_space=pltpu.VMEM)

    def call(body, outs, *args, placed=near, scratch=(), **static):
        return pl.pallas_call(
            lambda *refs: body(*refs, **static),
            out_shape=outs,
            in_specs=[vmem] * len(args),
            out_specs=[vmem] * len(outs),
            scratch_shapes=scratch,
        )(*map(placed, args))

    def exchanged(send, face):
        edge = lax.ppermute(face, "gy", facing)
        pair = lax.all_gather(send, ("gx", "gy"), axis_index_groups=columns, tiled=True)
        both = jnp.concatenate([pair, edge], axis=0)
        return lax.all_gather(both, "gy", axis_index_groups=mates, tiled=True)

    def among_chips(buffer):
        return lax.all_to_all(buffer, ("gx", "gy"), 0, 0, tiled=True, axis_index_groups=chips)

    small, large = call(
        pack_kernel, [result(8, 24, 128), result(8, 328, 128)], rhs_field, accumulation, trans_x, trans_y, trans_z,
        held_cells, perf_host, well_index, seg_cond, seg_rate, placed=lambda value: value,
    )
    fields = among_chips(large)
    message, edges, grid, wells = shape(96, 128), shape(32, 128), shape(64, 8, 128), shape(32, 128)
    send, face = call(share_kernel, [message, edges], among_chips(small))
    recv = exchanged(send, face)
    p, gain, wx, wy, seg, well, held, send, face = call(
        first_kernel,
        [grid, grid, shape(2, 8, 128), edges, wells, shape(4, 32, 128), pltpu.VMEM((8, 8, 128), jnp.int32), message, edges],
        fields, recv, scratch=[grid],
    )
    for sweep in range(1, SWEEPS):
        last = sweep == SWEEPS - 1
        recv = exchanged(send, face)
        outs = [result(8, 8, 128), result(1, 2, 128)] if last else [grid, wells, message, edges]
        got = call(
            sweep_kernel, outs, p, fields, gain, wx, wy, recv, seg, well, held,
            scratch=[grid, grid] if last else [grid], last=last,
        )
        p, seg = got[:2]
        if not last:
            send, face = got[2:]
    return (p, seg)


def solution(mesh):
    return jax.shard_map(
        shards,
        mesh=mesh,
        in_specs=(
            P("gx", "gy", None),
            P("gx", "gy", None),
            P("gx", "gy", None),
            P("gx", "gy", None),
            P("gx", "gy", None),
            P(None, "gx", "gy", None),
            P("gx", "gy", None),
            P("gx", "gy", None),
            P("gx", "gy", None),
            P("gx", "gy", None),
        ),
        out_specs=(P("gx", "gy", None), P("gx", "gy", None)),
        check_vma=False,
    )
```

```python
import jax
import jax.numpy as jnp
from jax import lax
from jax.experimental import pallas as pl
from jax.experimental.pallas import tpu as pltpu
from jax.sharding import PartitionSpec as P

SWEEPS = 6
F32 = jnp.float32
BF16 = jnp.bfloat16


def split3(value):
    high = value.astype(BF16)
    rest = value - high.astype(F32)
    middle = rest.astype(BF16)
    low = (rest - middle.astype(F32)).astype(BF16)
    return high, middle, low


def iota(shape, dim):
    return lax.broadcasted_iota(jnp.int32, shape, dim)


def lane_onehot(idx, lanes):
    lane_of = idx & (lanes - 1)
    pieces = []
    for row in range(idx.shape[0]):
        hit = iota((lanes, idx.shape[1]), 0) == lane_of[row : row + 1, :]
        pieces.append(jnp.where(hit, F32(1.0), F32(0.0)).astype(BF16))
    return jnp.concatenate(pieces, axis=1)


def row_hit(idx, row, lanes, count):
    shift = lanes.bit_length() - 1
    row_of = lax.shift_right_logical(idx[row : row + 1, :], shift)
    return iota((count, idx.shape[1]), 0) == row_of


def scatter(flux, idx, lane_hot, count, lanes):
    parts = [part.astype(F32) for part in split3(flux)]
    columns = []
    for row in range(idx.shape[0]):
        hit = row_hit(idx, row, lanes, count)
        columns.append(
            jnp.concatenate(
                [jnp.where(hit, part[row : row + 1, :], F32(0.0)).astype(BF16) for part in parts],
                axis=0,
            )
        )
    spread = jnp.concatenate(columns, axis=1)
    out = lax.dot_general(
        spread, lane_hot, (((1,), (1,)), ((), ())), preferred_element_type=F32
    )
    return out[:count] + out[count : 2 * count] + out[2 * count :]


def gather(cells, idx, lane_hot, lanes):
    count = cells.shape[0]
    stacked = jnp.concatenate(split3(cells), axis=0)
    picked = lax.dot_general(
        stacked, lane_hot, (((1,), (0,)), ((), ())), preferred_element_type=F32
    )
    picked = picked[:count] + picked[count : 2 * count] + picked[2 * count :]
    slots = idx.shape[1]
    out = jnp.zeros(idx.shape, F32)
    for row in range(idx.shape[0]):
        part = jnp.where(
            row_hit(idx, row, lanes, count), picked[:, row * slots : (row + 1) * slots], F32(0.0)
        )
        total = jnp.sum(part, axis=0, keepdims=True)
        out = jnp.where(iota(idx.shape, 0) == row, total, out)
    return out


def well_update(rate, index, fm, seg, cell_p):
    slots = seg.shape[1]
    fp = pltpu.roll(fm, slots - 1, 1)
    seg_prev = pltpu.roll(seg, 1, 1)
    seg_next = pltpu.roll(seg, slots - 1, 1)
    seg_res = rate - (
        index * (seg - cell_p) + fm * (seg - seg_prev) + fp * (seg - seg_next)
    )
    return seg + F32(0.8) * seg_res / (index + fm + fp)


UNIT = 4
PARTS = 48


def z_shifted(plane, step):
    size = plane.shape[1]
    moved = pltpu.roll(plane, (-step) % size, 1)
    at = size - 1 if step > 0 else 0
    return jnp.where(iota(plane.shape, 1) == at, F32(0.0), moved)


def y_moved(plane, edge, step):
    size = plane.shape[0]
    at = size - 1 if step > 0 else 0
    return jnp.where(iota(plane.shape, 0) == at, edge, pltpu.roll(plane, (-step) % size, 0))


def places():
    unit = lax.axis_index("gx") // UNIT
    odd = unit & 1
    half = 4 * PARTS + 8 * UNIT
    return unit, odd * 2 * PARTS, odd * half + 2 * PARTS, (1 - odd) * half


def rows_at(recv_ref, start, count=8):
    return recv_ref[pl.ds(pl.multiple_of(start, 8), count), :]


def lifted(piece, shift):
    tall = jnp.concatenate([piece, jnp.zeros_like(piece)], axis=0)
    shift = shift % tall.shape[0]
    return pltpu.roll(tall, shift, 0) if shift else tall


def window(rows, y, block):
    start = 16 * y + 6 - 2 * block
    moved = pltpu.roll(rows, (-start) % rows.shape[0], 0) if start else rows
    return moved[:8]


def spread_block(flux, host, held_ref, y, block):
    near_host = window(host, y, block)
    part = window(flux, y, block)
    part = jnp.where(near_host == (iota(part.shape, 0) // 2).astype(F32), part, F32(0.0))
    idx = held_ref[2 * block + y]
    hot = lane_onehot(idx, 128)
    return scatter(part, idx, hot, 64, 128), hot


def spread_wells(flux, host, held_ref, term_ref):
    hots = []
    for y in range(2):
        for block in range(UNIT):
            term, hot = spread_block(flux, host, held_ref, y, block)
            hots.append(hot)
            term_ref[pl.ds(32 * y + 8 * block, 8)] = term.reshape(8, 8, 128)
    return hots


def send_out(p_ref, held_ref, hots, send_ref, face_ref):
    for y in range(2):
        for block in range(UNIT):
            cells = p_ref[pl.ds(32 * y + 8 * block, 8)].reshape(64, 128)
            vals = gather(cells, held_ref[2 * block + y], hots[UNIT * y + block], 128)
            send_ref[pl.ds(PARTS * y + 8 * block, 8), :] = vals
        send_ref[pl.ds(PARTS * y + 32, 8), :] = p_ref[32 * y]
        send_ref[pl.ds(PARTS * y + 40, 8), :] = p_ref[32 * y + 31]
    upper = (lax.axis_index("gy") & 1) == 1
    for x in range(32):
        face_ref[x : x + 1, :] = jnp.where(upper, p_ref[32 + x, 7:8, :], p_ref[x, 0:1, :])


def field(fields_ref, which, y, x):
    return fields_ref[2 * (x // 8) + y, pl.ds(64 * which + 8 * (x % 8), 8), :]


def pack_kernel(
    rhs_ref, acc_ref, tx_ref, ty_ref, tz_ref, held_ref, host_ref, index_ref, cond_ref, rate_ref, small_ref, large_ref
):
    members = large_ref.shape[0]
    pack = jnp.concatenate(
        [host_ref[0].astype(F32), index_ref[0], cond_ref[0], rate_ref[0]], axis=0
    )
    edge = jnp.concatenate([ty_ref[x, 7:8, :] for x in range(8)], axis=0)
    for m in range(members):
        small_ref[m, 0:8, :] = pack
        small_ref[m, 8:16, :] = tx_ref[7]
        small_ref[m, 16:24, :] = edge
    for which, ref in enumerate((rhs_ref, acc_ref, tx_ref, ty_ref, tz_ref)):
        whole = ref[...].reshape(64, 128)
        for m in range(members):
            large_ref[m, 64 * which : 64 * which + 64, :] = whole
    held = held_ref[...].reshape(8, 128).astype(F32)
    for m in range(members):
        large_ref[m, 320:328, :] = held


def share_kernel(small_ref, send_ref, face_ref):
    for y in range(2):
        for block in range(UNIT):
            send_ref[pl.ds(PARTS * y + 8 * block, 8), :] = small_ref[2 * block + y, 0:8, :]
        send_ref[pl.ds(PARTS * y + 32, 8), :] = jnp.zeros((8, 128), F32)
        send_ref[pl.ds(PARTS * y + 40, 8), :] = small_ref[2 * (UNIT - 1) + y, 8:16, :]
    for block in range(UNIT):
        face_ref[pl.ds(8 * block, 8), :] = small_ref[2 * block + 1, 16:24, :]


def first_kernel(
    fields_ref, recv_ref, p_ref, coef_ref, wx_ref, wy_ref, seg_ref, well_ref, held_ref, send_ref, face_ref, term_ref
):
    unit, here, after, before = places()
    own = iota((16, 128), 0) // 2
    groups = []
    for array in range(4):
        halves = []
        for y in range(2):
            whole = jnp.zeros((16, 128), F32)
            for owner in range(-UNIT, UNIT):
                base = here + 8 * owner if owner >= 0 else before + 8 * (owner + UNIT)
                place = UNIT - 1 - owner
                moved = lifted(rows_at(recv_ref, base + PARTS * y), 2 * place - 2 * array)
                whole = jnp.where(own == place, moved, whole)
            halves.append(whole)
        groups.append(jnp.concatenate(halves, axis=0))
    host, index, cond, rate = groups
    fm = jnp.where(iota(cond.shape, 1) > 0, cond, F32(0.0))
    well_ref[0], well_ref[1], well_ref[2], well_ref[3] = host, index, fm, rate
    zero = jnp.zeros(cond.shape, F32)
    seg = well_update(rate, index, fm, zero, zero)
    seg_ref[...] = seg
    for m in range(2 * UNIT):
        held_ref[m] = fields_ref[m, 320:328, :].astype(jnp.int32)
    hots = spread_wells(F32(0.0) - index * seg, host, held_ref, term_ref)
    wy_ref[...] = recv_ref[4 * PARTS : 4 * PARTS + 32, :]
    top = iota((8, 128), 1) == 127
    for y in range(2):
        west = rows_at(recv_ref, before + PARTS * y + 40)
        west = jnp.where(unit == 0, F32(0.0), west)
        wx_ref[y] = west
        for x in range(32):
            tx, ty, tz = (field(fields_ref, which, y, x) for which in (2, 3, 4))
            edge = field(fields_ref, 3, 0, x)[7:8, :] if y else recv_ref[4 * PARTS + x : 4 * PARTS + x + 1, :]
            wx = field(fields_ref, 2, y, x - 1) if x else west
            wy = y_moved(ty, edge, -1)
            inner = jnp.where(top, F32(0.0), tz)
            wz = pltpu.roll(inner, 1, 1)
            gain = F32(0.7) / (field(fields_ref, 1, y, x) + tx + wx + ty + wy + tz + wz)
            base = gain * field(fields_ref, 0, y, x)
            at = 32 * y + x
            for which, value in enumerate((tx, ty, inner, gain, base)):
                coef_ref[which, at] = value
            p_ref[at] = base - gain * term_ref[at]
    send_out(p_ref, held_ref, hots, send_ref, face_ref)


def sweep_kernel(p_in, coef_ref, wx_ref, wy_ref, recv_ref, seg_in, well_ref, held_ref, *rest, last):
    if last:
        out_ref, seg_out = rest
    else:
        p_ref, seg_ref, send_ref, face_ref, term_ref = rest
    unit, here, after, before = places()
    units = lax.axis_size("gx") // UNIT
    host, index, fm, rate = well_ref[0], well_ref[1], well_ref[2], well_ref[3]
    own = iota((16, 128), 0) // 2
    halves = []
    for y in range(2):
        cell = jnp.zeros((16, 128), F32)
        near_host = host[16 * y : 16 * y + 16]
        for block in range(1 - UNIT, 2 * UNIT - 1):
            base = here if 0 <= block < UNIT else after if block > 0 else before
            vals = rows_at(recv_ref, base + PARTS * y + 8 * (block % UNIT))
            hit = near_host == (own + block - 3).astype(F32)
            cell = jnp.where(hit, lifted(vals, 6 - 2 * block), cell)
        halves.append(cell)
    cell_p = jnp.concatenate(halves, axis=0)
    seg = well_update(rate, index, fm, seg_in[...], cell_p)
    flux = index * (cell_p - seg)
    half = 4 * PARTS + 32
    lines = (slice(4 * PARTS, half), slice(half + 4 * PARTS, 2 * half))

    def updated(y, x, term):
        at = 32 * y + x
        block = p_in[at]
        if y:
            south, north = p_in[x, 7:8, :], recv_ref[lines[1].start + x : lines[1].start + x + 1, :]
        else:
            south, north = recv_ref[lines[0].start + x : lines[0].start + x + 1, :], p_in[32 + x, 0:1, :]
        if x < 31:
            east = p_in[at + 1]
        else:
            east = rows_at(recv_ref, after + PARTS * y + 32)
            east = jnp.where(unit == units - 1, F32(0.0), east)
        if x:
            west = p_in[at - 1]
        else:
            west = rows_at(recv_ref, before + PARTS * y + 40)
            west = jnp.where(unit == 0, F32(0.0), west)
        tx, ty, tz, gain, base = (coef_ref[which, at] for which in range(5))
        edge = coef_ref[1, x, 7:8, :] if y else wy_ref[x : x + 1, :]
        total = tx * east + (coef_ref[0, at - 1] if x else wx_ref[y]) * west
        total = total + ty * y_moved(block, north, 1) + y_moved(ty, edge, -1) * y_moved(block, south, -1)
        total = total + tz * pltpu.roll(block, 127, 1) + pltpu.roll(tz, 1, 1) * pltpu.roll(block, 1, 1)
        return F32(0.3) * block + base + gain * (total - term)

    if last:
        place = lax.axis_index("gx") % UNIT
        core = lax.axis_index("gy") & 1
        for y in range(2):
            for block in range(UNIT):

                @pl.when((place == block) & (core == y))
                def _(y=y, block=block):
                    term, _ = spread_block(flux, host, held_ref, y, block)
                    for x in range(8):
                        out_ref[x] = updated(y, 8 * block + x, term[8 * x : 8 * x + 8])
                    start = 16 * y + 2 * (UNIT - 1 - block)
                    seg_out[0] = seg[start : start + 2]

    else:
        hots = spread_wells(flux, host, held_ref, term_ref)
        for y in range(2):
            for x in range(32):
                p_ref[32 * y + x] = updated(y, x, term_ref[32 * y + x])
        seg_ref[...] = seg
        send_out(p_ref, held_ref, hots, send_ref, face_ref)


def shards(
    rhs_field,
    accumulation,
    trans_x,
    trans_y,
    trans_z,
    held_cells,
    perf_host,
    well_index,
    seg_cond,
    seg_rate,
):
    ring = lax.axis_size("gx")
    county = lax.axis_size("gy")
    units = ring // UNIT
    facing = [(j, j + 1) for j in range(1, county - 1, 2)]
    facing += [(target, source) for source, target in facing]
    mates = [[j, j + 1] for j in range(0, county, 2)]
    chips = [
        [(UNIT * unit + x) * county + j + core for x in range(UNIT) for core in range(2)]
        for unit in range(units)
        for j in range(0, county, 2)
    ]
    columns = [
        [(((low + step + j % 2) % units) * UNIT + x) * county + j for step in range(2)]
        for j in range(county)
        for low in range(0, units, 2)
        for x in range(UNIT)
    ]

    def shape(*dims):
        return pltpu.VMEM(dims, F32)

    def result(*dims):
        return jax.ShapeDtypeStruct(dims, F32)

    def near(value):
        return pltpu.with_memory_space_constraint(value, pltpu.VMEM)

    vmem = pl.BlockSpec(memory_space=pltpu.VMEM)

    def call(body, outs, *args, placed=near, scratch=(), **static):
        return pl.pallas_call(
            lambda *refs: body(*refs, **static),
            out_shape=outs,
            in_specs=[vmem] * len(args),
            out_specs=[vmem] * len(outs),
            scratch_shapes=scratch,
        )(*map(placed, args))

    def exchanged(send, face):
        edge = lax.ppermute(face, "gy", facing)
        pair = lax.all_gather(send, ("gx", "gy"), axis_index_groups=columns, tiled=True)
        both = jnp.concatenate([pair, edge], axis=0)
        return lax.all_gather(both, "gy", axis_index_groups=mates, tiled=True)

    def among_chips(buffer):
        return lax.all_to_all(buffer, ("gx", "gy"), 0, 0, tiled=True, axis_index_groups=chips)

    small, large = call(
        pack_kernel, [result(8, 24, 128), result(8, 328, 128)], rhs_field, accumulation, trans_x, trans_y, trans_z,
        held_cells, perf_host, well_index, seg_cond, seg_rate, placed=lambda value: value,
    )
    fields = among_chips(large)
    message, edges, grid, wells = shape(96, 128), shape(32, 128), shape(64, 8, 128), shape(32, 128)
    send, face = call(share_kernel, [message, edges], among_chips(small))
    recv = exchanged(send, face)
    p, coef, wx, wy, seg, well, held, send, face = call(
        first_kernel,
        [grid, shape(5, 64, 8, 128), shape(2, 8, 128), edges, wells, shape(4, 32, 128), pltpu.VMEM((8, 8, 128), jnp.int32), message, edges],
        fields, recv, scratch=[grid], placed=lambda value: value if value is fields else near(value),
    )
    for sweep in range(1, SWEEPS):
        last = sweep == SWEEPS - 1
        recv = exchanged(send, face)
        outs = [result(8, 8, 128), result(1, 2, 128)] if last else [grid, wells, message, edges]
        got = call(
            sweep_kernel, outs, p, coef, wx, wy, recv, seg, well, held, scratch=[] if last else [grid], last=last,
        )
        p, seg = got[:2]
        if not last:
            send, face = got[2:]
    return (p, seg)


def solution(mesh):
    return jax.shard_map(
        shards,
        mesh=mesh,
        in_specs=(
            P("gx", "gy", None),
            P("gx", "gy", None),
            P("gx", "gy", None),
            P("gx", "gy", None),
            P("gx", "gy", None),
            P(None, "gx", "gy", None),
            P("gx", "gy", None),
            P("gx", "gy", None),
            P("gx", "gy", None),
            P("gx", "gy", None),
        ),
        out_specs=(P("gx", "gy", None), P("gx", "gy", None)),
        check_vma=False,
    )
```

```python
import jax
import jax.numpy as jnp
from jax import lax
from jax.experimental import pallas as pl
from jax.experimental.pallas import tpu as pltpu
from jax.sharding import PartitionSpec as P

SWEEPS = 6
F32 = jnp.float32
BF16 = jnp.bfloat16


def split3(value):
    high = value.astype(BF16)
    rest = value - high.astype(F32)
    middle = rest.astype(BF16)
    low = (rest - middle.astype(F32)).astype(BF16)
    return high, middle, low


def iota(shape, dim):
    return lax.broadcasted_iota(jnp.int32, shape, dim)


def lane_onehot(idx, lanes):
    lane_of = idx & (lanes - 1)
    pieces = []
    for row in range(idx.shape[0]):
        hit = iota((lanes, idx.shape[1]), 0) == lane_of[row : row + 1, :]
        pieces.append(jnp.where(hit, F32(1.0), F32(0.0)).astype(BF16))
    return jnp.concatenate(pieces, axis=1)


def row_hit(idx, row, lanes, count):
    shift = lanes.bit_length() - 1
    row_of = lax.shift_right_logical(idx[row : row + 1, :], shift)
    return iota((count, idx.shape[1]), 0) == row_of


def scatter(flux, idx, lane_hot, count, lanes):
    parts = [part.astype(F32) for part in split3(flux)]
    columns = []
    for row in range(idx.shape[0]):
        hit = row_hit(idx, row, lanes, count)
        columns.append(
            jnp.concatenate(
                [jnp.where(hit, part[row : row + 1, :], F32(0.0)).astype(BF16) for part in parts],
                axis=0,
            )
        )
    spread = jnp.concatenate(columns, axis=1)
    out = lax.dot_general(
        spread, lane_hot, (((1,), (1,)), ((), ())), preferred_element_type=F32
    )
    return out[:count] + out[count : 2 * count] + out[2 * count :]


def gather(cells, idx, lane_hot, lanes):
    count = cells.shape[0]
    stacked = jnp.concatenate(split3(cells), axis=0)
    picked = lax.dot_general(
        stacked, lane_hot, (((1,), (0,)), ((), ())), preferred_element_type=F32
    )
    picked = picked[:count] + picked[count : 2 * count] + picked[2 * count :]
    slots = idx.shape[1]
    out = jnp.zeros(idx.shape, F32)
    for row in range(idx.shape[0]):
        part = jnp.where(
            row_hit(idx, row, lanes, count), picked[:, row * slots : (row + 1) * slots], F32(0.0)
        )
        total = jnp.sum(part, axis=0, keepdims=True)
        out = jnp.where(iota(idx.shape, 0) == row, total, out)
    return out


def well_update(rate, index, fm, seg, cell_p):
    slots = seg.shape[1]
    fp = pltpu.roll(fm, slots - 1, 1)
    seg_prev = pltpu.roll(seg, 1, 1)
    seg_next = pltpu.roll(seg, slots - 1, 1)
    seg_res = rate - (
        index * (seg - cell_p) + fm * (seg - seg_prev) + fp * (seg - seg_next)
    )
    return seg + F32(0.8) * seg_res / (index + fm + fp)


UNIT = 4
PARTS = 48


def z_shifted(plane, step):
    size = plane.shape[1]
    moved = pltpu.roll(plane, (-step) % size, 1)
    at = size - 1 if step > 0 else 0
    return jnp.where(iota(plane.shape, 1) == at, F32(0.0), moved)


def y_moved(plane, edge, step):
    size = plane.shape[0]
    at = size - 1 if step > 0 else 0
    return jnp.where(iota(plane.shape, 0) == at, edge, pltpu.roll(plane, (-step) % size, 0))


def places():
    unit = lax.axis_index("gx") // UNIT
    odd = unit & 1
    half = 4 * PARTS + 8 * UNIT
    return unit, odd * 2 * PARTS, odd * half + 2 * PARTS, (1 - odd) * half


def rows_at(recv_ref, start, count=8):
    return recv_ref[pl.ds(pl.multiple_of(start, 8), count), :]


def lifted(piece, shift):
    tall = jnp.concatenate([piece, jnp.zeros_like(piece)], axis=0)
    shift = shift % tall.shape[0]
    return pltpu.roll(tall, shift, 0) if shift else tall


def window(rows, y, block):
    start = 16 * y + 6 - 2 * block
    moved = pltpu.roll(rows, (-start) % rows.shape[0], 0) if start else rows
    return moved[:8]


def spread_block(flux, host, held_ref, y, block):
    near_host = window(host, y, block)
    part = window(flux, y, block)
    part = jnp.where(near_host == (iota(part.shape, 0) // 2).astype(F32), part, F32(0.0))
    idx = held_ref[2 * block + y]
    hot = lane_onehot(idx, 128)
    return scatter(part, idx, hot, 64, 128), hot


def spread_wells(flux, host, held_ref, term_ref):
    hots = []
    for y in range(2):
        for block in range(UNIT):
            term, hot = spread_block(flux, host, held_ref, y, block)
            hots.append(hot)
            term_ref[pl.ds(32 * y + 8 * block, 8)] = term.reshape(8, 8, 128)
    return hots


def send_out(p_ref, held_ref, hots, send_ref, face_ref):
    for y in range(2):
        for block in range(UNIT):
            cells = p_ref[pl.ds(32 * y + 8 * block, 8)].reshape(64, 128)
            vals = gather(cells, held_ref[2 * block + y], hots[UNIT * y + block], 128)
            send_ref[pl.ds(PARTS * y + 8 * block, 8), :] = vals
        send_ref[pl.ds(PARTS * y + 32, 8), :] = p_ref[32 * y]
        send_ref[pl.ds(PARTS * y + 40, 8), :] = p_ref[32 * y + 31]
    upper = (lax.axis_index("gy") & 1) == 1
    for x in range(32):
        face_ref[x : x + 1, :] = jnp.where(upper, p_ref[32 + x, 7:8, :], p_ref[x, 0:1, :])


def field(fields_ref, which, y, x):
    return fields_ref[2 * (x // 8) + y, pl.ds(64 * which + 8 * (x % 8), 8), :]


def pack_kernel(
    rhs_ref, acc_ref, tx_ref, ty_ref, tz_ref, held_ref, host_ref, index_ref, cond_ref, rate_ref, small_ref, large_ref
):
    members = large_ref.shape[0]
    pack = jnp.concatenate(
        [host_ref[0].astype(F32), index_ref[0], cond_ref[0], rate_ref[0]], axis=0
    )
    edge = jnp.concatenate([ty_ref[x, 7:8, :] for x in range(8)], axis=0)
    for m in range(members):
        small_ref[m, 0:8, :] = pack
        small_ref[m, 8:16, :] = tx_ref[7]
        small_ref[m, 16:24, :] = edge
    for which, ref in enumerate((rhs_ref, acc_ref, tx_ref, ty_ref, tz_ref)):
        whole = ref[...].reshape(64, 128)
        for m in range(members):
            large_ref[m, 64 * which : 64 * which + 64, :] = whole
    held = held_ref[...].reshape(8, 128).astype(F32)
    for m in range(members):
        large_ref[m, 320:328, :] = held


def share_kernel(small_ref, send_ref, face_ref):
    for y in range(2):
        for block in range(UNIT):
            send_ref[pl.ds(PARTS * y + 8 * block, 8), :] = small_ref[2 * block + y, 0:8, :]
        send_ref[pl.ds(PARTS * y + 32, 8), :] = jnp.zeros((8, 128), F32)
        send_ref[pl.ds(PARTS * y + 40, 8), :] = small_ref[2 * (UNIT - 1) + y, 8:16, :]
    for block in range(UNIT):
        face_ref[pl.ds(8 * block, 8), :] = small_ref[2 * block + 1, 16:24, :]


def first_kernel(
    fields_ref, recv_ref, p_ref, tx_out, ty_out, tz_out, gain_out, base_out, wx_ref, wy_ref, seg_ref, well_ref, held_ref, send_ref, face_ref, term_ref
):
    unit, here, after, before = places()
    own = iota((16, 128), 0) // 2
    groups = []
    for array in range(4):
        halves = []
        for y in range(2):
            whole = jnp.zeros((16, 128), F32)
            for owner in range(-UNIT, UNIT):
                base = here + 8 * owner if owner >= 0 else before + 8 * (owner + UNIT)
                place = UNIT - 1 - owner
                moved = lifted(rows_at(recv_ref, base + PARTS * y), 2 * place - 2 * array)
                whole = jnp.where(own == place, moved, whole)
            halves.append(whole)
        groups.append(jnp.concatenate(halves, axis=0))
    host, index, cond, rate = groups
    fm = jnp.where(iota(cond.shape, 1) > 0, cond, F32(0.0))
    well_ref[0], well_ref[1], well_ref[2], well_ref[3] = host, index, fm, rate
    zero = jnp.zeros(cond.shape, F32)
    seg = well_update(rate, index, fm, zero, zero)
    seg_ref[...] = seg
    for m in range(2 * UNIT):
        held_ref[m] = fields_ref[m, 320:328, :].astype(jnp.int32)
    hots = spread_wells(F32(0.0) - index * seg, host, held_ref, term_ref)
    wy_ref[...] = recv_ref[4 * PARTS : 4 * PARTS + 32, :]
    top = iota((8, 128), 1) == 127
    for y in range(2):
        west = rows_at(recv_ref, before + PARTS * y + 40)
        west = jnp.where(unit == 0, F32(0.0), west)
        wx_ref[y] = west
        for x in range(32):
            tx, ty, tz = (field(fields_ref, which, y, x) for which in (2, 3, 4))
            edge = field(fields_ref, 3, 0, x)[7:8, :] if y else recv_ref[4 * PARTS + x : 4 * PARTS + x + 1, :]
            wx = field(fields_ref, 2, y, x - 1) if x else west
            wy = y_moved(ty, edge, -1)
            inner = jnp.where(top, F32(0.0), tz)
            wz = pltpu.roll(inner, 1, 1)
            gain = F32(0.7) / (field(fields_ref, 1, y, x) + tx + wx + ty + wy + tz + wz)
            base = gain * field(fields_ref, 0, y, x)
            at = 32 * y + x
            tx_out[at], ty_out[at], tz_out[at], gain_out[at], base_out[at] = tx, ty, inner, gain, base
            p_ref[at] = base - gain * term_ref[at]
    send_out(p_ref, held_ref, hots, send_ref, face_ref)


def sweep_kernel(
    p_in, tx_ref, ty_ref, tz_ref, gain_ref, base_ref, wx_ref, wy_ref, recv_ref, seg_in, well_ref, held_ref, *rest, last
):
    if last:
        out_ref, seg_out = rest
    else:
        p_ref, seg_ref, send_ref, face_ref, term_ref = rest
    unit, here, after, before = places()
    units = lax.axis_size("gx") // UNIT
    host, index, fm, rate = well_ref[0], well_ref[1], well_ref[2], well_ref[3]
    own = iota((16, 128), 0) // 2
    halves = []
    for y in range(2):
        cell = jnp.zeros((16, 128), F32)
        near_host = host[16 * y : 16 * y + 16]
        for block in range(1 - UNIT, 2 * UNIT - 1):
            base = here if 0 <= block < UNIT else after if block > 0 else before
            vals = rows_at(recv_ref, base + PARTS * y + 8 * (block % UNIT))
            hit = near_host == (own + block - 3).astype(F32)
            cell = jnp.where(hit, lifted(vals, 6 - 2 * block), cell)
        halves.append(cell)
    cell_p = jnp.concatenate(halves, axis=0)
    seg = well_update(rate, index, fm, seg_in[...], cell_p)
    flux = index * (cell_p - seg)
    half = 4 * PARTS + 32
    lines = (slice(4 * PARTS, half), slice(half + 4 * PARTS, 2 * half))

    def updated(y, x, term):
        at = 32 * y + x
        block = p_in[at]
        if y:
            south, north = p_in[x, 7:8, :], recv_ref[lines[1].start + x : lines[1].start + x + 1, :]
        else:
            south, north = recv_ref[lines[0].start + x : lines[0].start + x + 1, :], p_in[32 + x, 0:1, :]
        if x < 31:
            east = p_in[at + 1]
        else:
            east = rows_at(recv_ref, after + PARTS * y + 32)
            east = jnp.where(unit == units - 1, F32(0.0), east)
        if x:
            west = p_in[at - 1]
        else:
            west = rows_at(recv_ref, before + PARTS * y + 40)
            west = jnp.where(unit == 0, F32(0.0), west)
        tx, ty, tz = tx_ref[at], ty_ref[at], tz_ref[at]
        edge = ty_ref[x, 7:8, :] if y else wy_ref[x : x + 1, :]
        total = tx * east + (tx_ref[at - 1] if x else wx_ref[y]) * west
        total = total + ty * y_moved(block, north, 1) + y_moved(ty, edge, -1) * y_moved(block, south, -1)
        total = total + tz * pltpu.roll(block, 127, 1) + pltpu.roll(tz, 1, 1) * pltpu.roll(block, 1, 1)
        return F32(0.3) * block + base_ref[at] + gain_ref[at] * (total - term)

    if last:
        place = lax.axis_index("gx") % UNIT
        core = lax.axis_index("gy") & 1
        for y in range(2):
            for block in range(UNIT):

                @pl.when((place == block) & (core == y))
                def _(y=y, block=block):
                    term, _ = spread_block(flux, host, held_ref, y, block)
                    for x in range(8):
                        out_ref[x] = updated(y, 8 * block + x, term[8 * x : 8 * x + 8])
                    start = 16 * y + 2 * (UNIT - 1 - block)
                    seg_out[0] = seg[start : start + 2]

    else:
        hots = spread_wells(flux, host, held_ref, term_ref)
        for y in range(2):
            for x in range(32):
                p_ref[32 * y + x] = updated(y, x, term_ref[32 * y + x])
        seg_ref[...] = seg
        send_out(p_ref, held_ref, hots, send_ref, face_ref)


def shards(
    rhs_field,
    accumulation,
    trans_x,
    trans_y,
    trans_z,
    held_cells,
    perf_host,
    well_index,
    seg_cond,
    seg_rate,
):
    ring = lax.axis_size("gx")
    county = lax.axis_size("gy")
    units = ring // UNIT
    facing = [(j, j + 1) for j in range(1, county - 1, 2)]
    facing += [(target, source) for source, target in facing]
    mates = [[j, j + 1] for j in range(0, county, 2)]
    chips = [
        [(UNIT * unit + x) * county + j + core for x in range(UNIT) for core in range(2)]
        for unit in range(units)
        for j in range(0, county, 2)
    ]
    columns = [
        [(((low + step + j % 2) % units) * UNIT + x) * county + j for step in range(2)]
        for j in range(county)
        for low in range(0, units, 2)
        for x in range(UNIT)
    ]

    def shape(*dims):
        return pltpu.VMEM(dims, F32)

    def result(*dims):
        return jax.ShapeDtypeStruct(dims, F32)

    def near(value):
        return pltpu.with_memory_space_constraint(value, pltpu.VMEM)

    vmem = pl.BlockSpec(memory_space=pltpu.VMEM)

    def call(body, outs, *args, placed=near, scratch=(), **static):
        return pl.pallas_call(
            lambda *refs: body(*refs, **static),
            out_shape=outs,
            in_specs=[vmem] * len(args),
            out_specs=[vmem] * len(outs),
            scratch_shapes=scratch,
        )(*map(placed, args))

    def exchanged(send, face):
        edge = lax.ppermute(face, "gy", facing)
        pair = lax.all_gather(send, ("gx", "gy"), axis_index_groups=columns, tiled=True)
        both = jnp.concatenate([pair, edge], axis=0)
        return lax.all_gather(both, "gy", axis_index_groups=mates, tiled=True)

    def among_chips(buffer):
        return lax.all_to_all(buffer, ("gx", "gy"), 0, 0, tiled=True, axis_index_groups=chips)

    small, large = call(
        pack_kernel, [result(8, 24, 128), result(8, 328, 128)], rhs_field, accumulation, trans_x, trans_y, trans_z,
        held_cells, perf_host, well_index, seg_cond, seg_rate, placed=lambda value: value,
    )
    fields = among_chips(large)
    message, edges, grid, wells = shape(96, 128), shape(32, 128), shape(64, 8, 128), shape(32, 128)
    send, face = call(share_kernel, [message, edges], among_chips(small))
    recv = exchanged(send, face)
    p, *kept, seg, well, held, send, face = call(
        first_kernel,
        [grid] * 6 + [shape(2, 8, 128), edges, wells, shape(4, 32, 128), pltpu.VMEM((8, 8, 128), jnp.int32), message, edges],
        fields, recv, scratch=[grid], placed=lambda value: value if value is fields else near(value),
    )
    for sweep in range(1, SWEEPS):
        last = sweep == SWEEPS - 1
        recv = exchanged(send, face)
        outs = [result(8, 8, 128), result(1, 2, 128)] if last else [grid, wells, message, edges]
        got = call(
            sweep_kernel, outs, p, *kept, recv, seg, well, held, scratch=[] if last else [grid], last=last,
        )
        p, seg = got[:2]
        if not last:
            send, face = got[2:]
    return (p, seg)


def solution(mesh):
    return jax.shard_map(
        shards,
        mesh=mesh,
        in_specs=(
            P("gx", "gy", None),
            P("gx", "gy", None),
            P("gx", "gy", None),
            P("gx", "gy", None),
            P("gx", "gy", None),
            P(None, "gx", "gy", None),
            P("gx", "gy", None),
            P("gx", "gy", None),
            P("gx", "gy", None),
            P("gx", "gy", None),
        ),
        out_specs=(P("gx", "gy", None), P("gx", "gy", None)),
        check_vma=False,
    )
```

```python
import jax
import jax.numpy as jnp
from jax import lax
from jax.experimental import pallas as pl
from jax.experimental.pallas import tpu as pltpu
from jax.sharding import PartitionSpec as P

SWEEPS = 6
F32 = jnp.float32
BF16 = jnp.bfloat16


def split(value):
    high = value.astype(BF16)
    return high, (value - high.astype(F32)).astype(BF16)


def iota(shape, dim):
    return lax.broadcasted_iota(jnp.int32, shape, dim)


def lane_onehot(idx, lanes):
    lane_of = idx & (lanes - 1)
    pieces = []
    for row in range(idx.shape[0]):
        hit = iota((lanes, idx.shape[1]), 0) == lane_of[row : row + 1, :]
        pieces.append(jnp.where(hit, F32(1.0), F32(0.0)).astype(BF16))
    return jnp.concatenate(pieces, axis=1)


def row_hit(idx, row, lanes, count):
    shift = lanes.bit_length() - 1
    row_of = lax.shift_right_logical(idx[row : row + 1, :], shift)
    return iota((count, idx.shape[1]), 0) == row_of


def scatter(flux, idx, lane_hot, count, lanes):
    parts = [part.astype(F32) for part in split(flux)]
    columns = []
    for row in range(idx.shape[0]):
        hit = row_hit(idx, row, lanes, count)
        columns.append(
            jnp.concatenate(
                [jnp.where(hit, part[row : row + 1, :], F32(0.0)).astype(BF16) for part in parts],
                axis=0,
            )
        )
    spread = jnp.concatenate(columns, axis=1)
    out = lax.dot_general(
        spread, lane_hot, (((1,), (1,)), ((), ())), preferred_element_type=F32
    )
    return out[:count] + out[count:]


def gather(cells, idx, lane_hot, lanes):
    count = cells.shape[0]
    stacked = jnp.concatenate(split(cells), axis=0)
    picked = lax.dot_general(
        stacked, lane_hot, (((1,), (0,)), ((), ())), preferred_element_type=F32
    )
    picked = picked[:count] + picked[count:]
    slots = idx.shape[1]
    out = jnp.zeros(idx.shape, F32)
    for row in range(idx.shape[0]):
        part = jnp.where(
            row_hit(idx, row, lanes, count), picked[:, row * slots : (row + 1) * slots], F32(0.0)
        )
        total = jnp.sum(part, axis=0, keepdims=True)
        out = jnp.where(iota(idx.shape, 0) == row, total, out)
    return out


def well_update(rate, index, fm, seg, cell_p):
    slots = seg.shape[1]
    fp = pltpu.roll(fm, slots - 1, 1)
    seg_prev = pltpu.roll(seg, 1, 1)
    seg_next = pltpu.roll(seg, slots - 1, 1)
    seg_res = rate - (
        index * (seg - cell_p) + fm * (seg - seg_prev) + fp * (seg - seg_next)
    )
    return seg + F32(0.8) * seg_res / (index + fm + fp)


UNIT = 4
PARTS = 48


def z_shifted(plane, step):
    size = plane.shape[1]
    moved = pltpu.roll(plane, (-step) % size, 1)
    at = size - 1 if step > 0 else 0
    return jnp.where(iota(plane.shape, 1) == at, F32(0.0), moved)


def y_moved(plane, edge, step):
    size = plane.shape[0]
    at = size - 1 if step > 0 else 0
    return jnp.where(iota(plane.shape, 0) == at, edge, pltpu.roll(plane, (-step) % size, 0))


def places():
    unit = lax.axis_index("gx") // UNIT
    odd = unit & 1
    half = 4 * PARTS + 8 * UNIT
    return unit, odd * 2 * PARTS, odd * half + 2 * PARTS, (1 - odd) * half


def rows_at(recv_ref, start, count=8):
    return recv_ref[pl.ds(pl.multiple_of(start, 8), count), :]


def lifted(piece, shift):
    tall = jnp.concatenate([piece, jnp.zeros_like(piece)], axis=0)
    shift = shift % tall.shape[0]
    return pltpu.roll(tall, shift, 0) if shift else tall


def window(rows, y, block):
    start = 16 * y + 6 - 2 * block
    moved = pltpu.roll(rows, (-start) % rows.shape[0], 0) if start else rows
    return moved[:8]


def spread_block(flux, host, held_ref, y, block):
    near_host = window(host, y, block)
    part = window(flux, y, block)
    part = jnp.where(near_host == (iota(part.shape, 0) // 2).astype(F32), part, F32(0.0))
    idx = held_ref[2 * block + y]
    hot = lane_onehot(idx, 128)
    return scatter(part, idx, hot, 64, 128), hot


def spread_wells(flux, host, held_ref, term_ref):
    hots = []
    for y in range(2):
        for block in range(UNIT):
            term, hot = spread_block(flux, host, held_ref, y, block)
            hots.append(hot)
            term_ref[pl.ds(32 * y + 8 * block, 8)] = term.reshape(8, 8, 128)
    return hots


def send_out(p_ref, held_ref, hots, send_ref, face_ref):
    for y in range(2):
        for block in range(UNIT):
            cells = p_ref[pl.ds(32 * y + 8 * block, 8)].reshape(64, 128)
            vals = gather(cells, held_ref[2 * block + y], hots[UNIT * y + block], 128)
            send_ref[pl.ds(PARTS * y + 8 * block, 8), :] = vals
        send_ref[pl.ds(PARTS * y + 32, 8), :] = p_ref[32 * y]
        send_ref[pl.ds(PARTS * y + 40, 8), :] = p_ref[32 * y + 31]
    upper = (lax.axis_index("gy") & 1) == 1
    for x in range(32):
        face_ref[x : x + 1, :] = jnp.where(upper, p_ref[32 + x, 7:8, :], p_ref[x, 0:1, :])


def field(fields_ref, which, y, x):
    return fields_ref[2 * (x // 8) + y, pl.ds(64 * which + 8 * (x % 8), 8), :]


def pack_kernel(
    rhs_ref, acc_ref, tx_ref, ty_ref, tz_ref, held_ref, host_ref, index_ref, cond_ref, rate_ref, small_ref, large_ref
):
    members = large_ref.shape[0]
    pack = jnp.concatenate(
        [host_ref[0].astype(F32), index_ref[0], cond_ref[0], rate_ref[0]], axis=0
    )
    edge = jnp.concatenate([ty_ref[x, 7:8, :] for x in range(8)], axis=0)
    for m in range(members):
        small_ref[m, 0:8, :] = pack
        small_ref[m, 8:16, :] = tx_ref[7]
        small_ref[m, 16:24, :] = edge
    for which, ref in enumerate((rhs_ref, acc_ref, tx_ref, ty_ref, tz_ref)):
        whole = ref[...].reshape(64, 128)
        for m in range(members):
            large_ref[m, 64 * which : 64 * which + 64, :] = whole
    held = held_ref[...].reshape(8, 128).astype(F32)
    for m in range(members):
        large_ref[m, 320:328, :] = held


def share_kernel(small_ref, send_ref, face_ref):
    for y in range(2):
        for block in range(UNIT):
            send_ref[pl.ds(PARTS * y + 8 * block, 8), :] = small_ref[2 * block + y, 0:8, :]
        send_ref[pl.ds(PARTS * y + 32, 8), :] = jnp.zeros((8, 128), F32)
        send_ref[pl.ds(PARTS * y + 40, 8), :] = small_ref[2 * (UNIT - 1) + y, 8:16, :]
    for block in range(UNIT):
        face_ref[pl.ds(8 * block, 8), :] = small_ref[2 * block + 1, 16:24, :]


def first_kernel(
    shared_ref, recv_ref, p_ref, tx_out, ty_out, tz_out, gain_out, base_out, wx_ref, wy_ref, seg_ref, well_ref, held_ref, send_ref, face_ref, term_ref, fields_ref, sem
):
    tail, body = pl.ds(320, 8), pl.ds(0, 320)
    late = pltpu.make_async_copy(shared_ref.at[:, tail], fields_ref.at[:, tail], sem.at[0])
    main = pltpu.make_async_copy(shared_ref.at[:, body], fields_ref.at[:, body], sem.at[1])
    late.start()
    main.start()
    unit, here, after, before = places()
    own = iota((16, 128), 0) // 2
    groups = []
    for array in range(4):
        halves = []
        for y in range(2):
            whole = jnp.zeros((16, 128), F32)
            for owner in range(-UNIT, UNIT):
                base = here + 8 * owner if owner >= 0 else before + 8 * (owner + UNIT)
                place = UNIT - 1 - owner
                moved = lifted(rows_at(recv_ref, base + PARTS * y), 2 * place - 2 * array)
                whole = jnp.where(own == place, moved, whole)
            halves.append(whole)
        groups.append(jnp.concatenate(halves, axis=0))
    host, index, cond, rate = groups
    fm = jnp.where(iota(cond.shape, 1) > 0, cond, F32(0.0))
    well_ref[0], well_ref[1], well_ref[2], well_ref[3] = host, index, fm, rate
    zero = jnp.zeros(cond.shape, F32)
    seg = well_update(rate, index, fm, zero, zero)
    seg_ref[...] = seg
    late.wait()
    for m in range(2 * UNIT):
        held_ref[m] = fields_ref[m, 320:328, :].astype(jnp.int32)
    hots = spread_wells(F32(0.0) - index * seg, host, held_ref, term_ref)
    wy_ref[...] = recv_ref[4 * PARTS : 4 * PARTS + 32, :]
    main.wait()
    top = iota((8, 128), 1) == 127
    for y in range(2):
        west = rows_at(recv_ref, before + PARTS * y + 40)
        west = jnp.where(unit == 0, F32(0.0), west)
        wx_ref[y] = west
        for x in range(32):
            tx, ty, tz = (field(fields_ref, which, y, x) for which in (2, 3, 4))
            edge = field(fields_ref, 3, 0, x)[7:8, :] if y else recv_ref[4 * PARTS + x : 4 * PARTS + x + 1, :]
            wx = field(fields_ref, 2, y, x - 1) if x else west
            wy = y_moved(ty, edge, -1)
            inner = jnp.where(top, F32(0.0), tz)
            wz = pltpu.roll(inner, 1, 1)
            gain = F32(0.7) / (field(fields_ref, 1, y, x) + tx + wx + ty + wy + tz + wz)
            base = gain * field(fields_ref, 0, y, x)
            at = 32 * y + x
            tx_out[at], ty_out[at], tz_out[at], gain_out[at], base_out[at] = tx, ty, inner, gain, base
            p_ref[at] = base - gain * term_ref[at]
    send_out(p_ref, held_ref, hots, send_ref, face_ref)


def sweep_kernel(
    p_in, tx_ref, ty_ref, tz_ref, gain_ref, base_ref, wx_ref, wy_ref, recv_ref, seg_in, well_ref, held_ref, *rest, last
):
    if last:
        out_ref, seg_out = rest
    else:
        p_ref, seg_ref, send_ref, face_ref, term_ref = rest
    unit, here, after, before = places()
    units = lax.axis_size("gx") // UNIT
    host, index, fm, rate = well_ref[0], well_ref[1], well_ref[2], well_ref[3]
    own = iota((16, 128), 0) // 2
    halves = []
    for y in range(2):
        cell = jnp.zeros((16, 128), F32)
        near_host = host[16 * y : 16 * y + 16]
        for block in range(1 - UNIT, 2 * UNIT - 1):
            base = here if 0 <= block < UNIT else after if block > 0 else before
            vals = rows_at(recv_ref, base + PARTS * y + 8 * (block % UNIT))
            hit = near_host == (own + block - 3).astype(F32)
            cell = jnp.where(hit, lifted(vals, 6 - 2 * block), cell)
        halves.append(cell)
    cell_p = jnp.concatenate(halves, axis=0)
    seg = well_update(rate, index, fm, seg_in[...], cell_p)
    flux = index * (cell_p - seg)
    half = 4 * PARTS + 32
    lines = (slice(4 * PARTS, half), slice(half + 4 * PARTS, 2 * half))

    def updated(y, x, term):
        at = 32 * y + x
        block = p_in[at]
        if y:
            south, north = p_in[x, 7:8, :], recv_ref[lines[1].start + x : lines[1].start + x + 1, :]
        else:
            south, north = recv_ref[lines[0].start + x : lines[0].start + x + 1, :], p_in[32 + x, 0:1, :]
        if x < 31:
            east = p_in[at + 1]
        else:
            east = rows_at(recv_ref, after + PARTS * y + 32)
            east = jnp.where(unit == units - 1, F32(0.0), east)
        if x:
            west = p_in[at - 1]
        else:
            west = rows_at(recv_ref, before + PARTS * y + 40)
            west = jnp.where(unit == 0, F32(0.0), west)
        tx, ty, tz = tx_ref[at], ty_ref[at], tz_ref[at]
        edge = ty_ref[x, 7:8, :] if y else wy_ref[x : x + 1, :]
        total = tx * east + (tx_ref[at - 1] if x else wx_ref[y]) * west
        total = total + ty * y_moved(block, north, 1) + y_moved(ty, edge, -1) * y_moved(block, south, -1)
        total = total + tz * pltpu.roll(block, 127, 1) + pltpu.roll(tz, 1, 1) * pltpu.roll(block, 1, 1)
        return F32(0.3) * block + base_ref[at] + gain_ref[at] * (total - term)

    if last:
        place = lax.axis_index("gx") % UNIT
        core = lax.axis_index("gy") & 1
        for y in range(2):
            for block in range(UNIT):

                @pl.when((place == block) & (core == y))
                def _(y=y, block=block):
                    term, _ = spread_block(flux, host, held_ref, y, block)
                    for x in range(8):
                        out_ref[x] = updated(y, 8 * block + x, term[8 * x : 8 * x + 8])
                    start = 16 * y + 2 * (UNIT - 1 - block)
                    seg_out[0] = seg[start : start + 2]

    else:
        hots = spread_wells(flux, host, held_ref, term_ref)
        for y in range(2):
            for x in range(32):
                p_ref[32 * y + x] = updated(y, x, term_ref[32 * y + x])
        seg_ref[...] = seg
        send_out(p_ref, held_ref, hots, send_ref, face_ref)


def shards(
    rhs_field,
    accumulation,
    trans_x,
    trans_y,
    trans_z,
    held_cells,
    perf_host,
    well_index,
    seg_cond,
    seg_rate,
):
    ring = lax.axis_size("gx")
    county = lax.axis_size("gy")
    units = ring // UNIT
    facing = [(j, j + 1) for j in range(1, county - 1, 2)]
    facing += [(target, source) for source, target in facing]
    mates = [[j, j + 1] for j in range(0, county, 2)]
    chips = [
        [(UNIT * unit + x) * county + j + core for x in range(UNIT) for core in range(2)]
        for unit in range(units)
        for j in range(0, county, 2)
    ]
    columns = [
        [(((low + step + j % 2) % units) * UNIT + x) * county + j for step in range(2)]
        for j in range(county)
        for low in range(0, units, 2)
        for x in range(UNIT)
    ]

    def shape(*dims):
        return pltpu.VMEM(dims, F32)

    def result(*dims):
        return jax.ShapeDtypeStruct(dims, F32)

    def near(value):
        return pltpu.with_memory_space_constraint(value, pltpu.VMEM)

    vmem = pl.BlockSpec(memory_space=pltpu.VMEM)

    def call(body, outs, *args, placed=near, scratch=(), specs=None, **static):
        return pl.pallas_call(
            lambda *refs: body(*refs, **static),
            out_shape=outs,
            in_specs=[vmem] * len(args) if specs is None else specs,
            out_specs=[vmem] * len(outs),
            scratch_shapes=scratch,
        )(*map(placed, args))

    def exchanged(send, face):
        edge = lax.ppermute(face, "gy", facing)
        pair = lax.all_gather(send, ("gx", "gy"), axis_index_groups=columns, tiled=True)
        both = jnp.concatenate([pair, edge], axis=0)
        return lax.all_gather(both, "gy", axis_index_groups=mates, tiled=True)

    def among_chips(buffer):
        return lax.all_to_all(buffer, ("gx", "gy"), 0, 0, tiled=True, axis_index_groups=chips)

    small, large = call(
        pack_kernel, [result(8, 24, 128), result(8, 328, 128)], rhs_field, accumulation, trans_x, trans_y, trans_z,
        held_cells, perf_host, well_index, seg_cond, seg_rate, placed=lambda value: value,
    )
    fields = among_chips(large)
    message, edges, grid, wells = shape(96, 128), shape(32, 128), shape(64, 8, 128), shape(32, 128)
    send, face = call(share_kernel, [message, edges], among_chips(small))
    recv = exchanged(send, face)
    p, *kept, seg, well, held, send, face = call(
        first_kernel,
        [grid] * 6 + [shape(2, 8, 128), edges, wells, shape(4, 32, 128), pltpu.VMEM((8, 8, 128), jnp.int32), message, edges],
        fields, recv, scratch=[grid, shape(8, 328, 128), pltpu.SemaphoreType.DMA((2,))],
        specs=[pl.BlockSpec(memory_space=pl.ANY), vmem], placed=lambda value: value if value is fields else near(value),
    )
    for sweep in range(1, SWEEPS):
        last = sweep == SWEEPS - 1
        recv = exchanged(send, face)
        outs = [result(8, 8, 128), result(1, 2, 128)] if last else [grid, wells, message, edges]
        got = call(
            sweep_kernel, outs, p, *kept, recv, seg, well, held, scratch=[] if last else [grid], last=last,
        )
        p, seg = got[:2]
        if not last:
            send, face = got[2:]
    return (p, seg)


def solution(mesh):
    return jax.shard_map(
        shards,
        mesh=mesh,
        in_specs=(
            P("gx", "gy", None),
            P("gx", "gy", None),
            P("gx", "gy", None),
            P("gx", "gy", None),
            P("gx", "gy", None),
            P(None, "gx", "gy", None),
            P("gx", "gy", None),
            P("gx", "gy", None),
            P("gx", "gy", None),
            P("gx", "gy", None),
        ),
        out_specs=(P("gx", "gy", None), P("gx", "gy", None)),
        check_vma=False,
    )
```

```python
import jax
import jax.numpy as jnp
from jax import lax
from jax.experimental import pallas as pl
from jax.experimental.pallas import tpu as pltpu
from jax.sharding import PartitionSpec as P

SWEEPS = 6
F32 = jnp.float32
BF16 = jnp.bfloat16


def split(value):
    high = value.astype(BF16)
    return high, (value - high.astype(F32)).astype(BF16)


def iota(shape, dim):
    return lax.broadcasted_iota(jnp.int32, shape, dim)


def lane_onehot(idx, lanes):
    lane_of = idx & (lanes - 1)
    pieces = []
    for row in range(idx.shape[0]):
        hit = iota((lanes, idx.shape[1]), 0) == lane_of[row : row + 1, :]
        pieces.append(jnp.where(hit, F32(1.0), F32(0.0)).astype(BF16))
    return jnp.concatenate(pieces, axis=1)


def row_hit(idx, row, lanes, count):
    shift = lanes.bit_length() - 1
    row_of = lax.shift_right_logical(idx[row : row + 1, :], shift)
    return iota((count, idx.shape[1]), 0) == row_of


def scatter(flux, idx, lane_hot, count, lanes):
    parts = [part.astype(F32) for part in split(flux)]
    columns = []
    for row in range(idx.shape[0]):
        hit = row_hit(idx, row, lanes, count)
        columns.append(
            jnp.concatenate(
                [jnp.where(hit, part[row : row + 1, :], F32(0.0)).astype(BF16) for part in parts],
                axis=0,
            )
        )
    spread = jnp.concatenate(columns, axis=1)
    out = lax.dot_general(
        spread, lane_hot, (((1,), (1,)), ((), ())), preferred_element_type=F32
    )
    return out[:count] + out[count:]


def gather(cells, idx, lane_hot, lanes):
    count = cells.shape[0]
    stacked = jnp.concatenate(split(cells), axis=0)
    picked = lax.dot_general(
        stacked, lane_hot, (((1,), (0,)), ((), ())), preferred_element_type=F32
    )
    picked = picked[:count] + picked[count:]
    slots = idx.shape[1]
    out = jnp.zeros(idx.shape, F32)
    for row in range(idx.shape[0]):
        part = jnp.where(
            row_hit(idx, row, lanes, count), picked[:, row * slots : (row + 1) * slots], F32(0.0)
        )
        total = jnp.sum(part, axis=0, keepdims=True)
        out = jnp.where(iota(idx.shape, 0) == row, total, out)
    return out


def well_update(rate, index, fm, seg, cell_p):
    slots = seg.shape[1]
    fp = pltpu.roll(fm, slots - 1, 1)
    seg_prev = pltpu.roll(seg, 1, 1)
    seg_next = pltpu.roll(seg, slots - 1, 1)
    seg_res = rate - (
        index * (seg - cell_p) + fm * (seg - seg_prev) + fp * (seg - seg_next)
    )
    return seg + F32(0.8) * seg_res / (index + fm + fp)


UNIT = 4
PARTS = 48


def z_shifted(plane, step):
    size = plane.shape[1]
    moved = pltpu.roll(plane, (-step) % size, 1)
    at = size - 1 if step > 0 else 0
    return jnp.where(iota(plane.shape, 1) == at, F32(0.0), moved)


def y_moved(plane, edge, step):
    size = plane.shape[0]
    at = size - 1 if step > 0 else 0
    return jnp.where(iota(plane.shape, 0) == at, edge, pltpu.roll(plane, (-step) % size, 0))


def places():
    unit = lax.axis_index("gx") // UNIT
    odd = unit & 1
    half = 4 * PARTS + 8 * UNIT
    return unit, odd * 2 * PARTS, odd * half + 2 * PARTS, (1 - odd) * half


def rows_at(recv_ref, start, count=8):
    return recv_ref[pl.ds(pl.multiple_of(start, 8), count), :]


def lifted(piece, shift):
    tall = jnp.concatenate([piece, jnp.zeros_like(piece)], axis=0)
    shift = shift % tall.shape[0]
    return pltpu.roll(tall, shift, 0) if shift else tall


def window(rows, y, block):
    start = 16 * y + 6 - 2 * block
    moved = pltpu.roll(rows, (-start) % rows.shape[0], 0) if start else rows
    return moved[:8]


def spread_block(flux, host, held_ref, y, block):
    near_host = window(host, y, block)
    part = window(flux, y, block)
    part = jnp.where(near_host == (iota(part.shape, 0) // 2).astype(F32), part, F32(0.0))
    idx = held_ref[2 * block + y]
    hot = lane_onehot(idx, 128)
    return scatter(part, idx, hot, 64, 128), hot


def spread_wells(flux, host, held_ref, term_ref):
    hots = []
    for y in range(2):
        for block in range(UNIT):
            term, hot = spread_block(flux, host, held_ref, y, block)
            hots.append(hot)
            term_ref[pl.ds(32 * y + 8 * block, 8)] = term.reshape(8, 8, 128)
    return hots


def send_out(p_ref, held_ref, hots, send_ref, face_ref):
    for y in range(2):
        for block in range(UNIT):
            cells = p_ref[pl.ds(32 * y + 8 * block, 8)].reshape(64, 128)
            vals = gather(cells, held_ref[2 * block + y], hots[UNIT * y + block], 128)
            send_ref[pl.ds(PARTS * y + 8 * block, 8), :] = vals
        send_ref[pl.ds(PARTS * y + 32, 8), :] = p_ref[32 * y]
        send_ref[pl.ds(PARTS * y + 40, 8), :] = p_ref[32 * y + 31]
    upper = (lax.axis_index("gy") & 1) == 1
    for x in range(32):
        face_ref[x : x + 1, :] = jnp.where(upper, p_ref[32 + x, 7:8, :], p_ref[x, 0:1, :])


def field(fields_ref, which, y, x):
    return fields_ref[2 * (x // 8) + y, pl.ds(64 * which + 8 * (x % 8), 8), :]


def pack_kernel(
    rhs_ref, acc_ref, tx_ref, ty_ref, tz_ref, held_ref, host_ref, index_ref, cond_ref, rate_ref, small_ref, large_ref
):
    members = large_ref.shape[0]
    pack = jnp.concatenate(
        [host_ref[0].astype(F32), index_ref[0], cond_ref[0], rate_ref[0]], axis=0
    )
    edge = jnp.concatenate([ty_ref[x, 7:8, :] for x in range(8)], axis=0)
    held = held_ref[...].reshape(8, 128).astype(F32)
    for m in range(members):
        small_ref[m, 0:8, :] = pack
        small_ref[m, 24:32, :] = held
        large_ref[m, 320:328, :] = held
        small_ref[m, 8:16, :] = tx_ref[7]
        small_ref[m, 16:24, :] = edge
    for which, ref in enumerate((rhs_ref, acc_ref, tx_ref, ty_ref, tz_ref)):
        whole = ref[...].reshape(64, 128)
        for m in range(members):
            large_ref[m, 64 * which : 64 * which + 64, :] = whole


def share_kernel(small_ref, send_ref, face_ref, held_ref):
    for m in range(2 * UNIT):
        held_ref[m] = small_ref[m, 24:32, :].astype(jnp.int32)
    for y in range(2):
        for block in range(UNIT):
            send_ref[pl.ds(PARTS * y + 8 * block, 8), :] = small_ref[2 * block + y, 0:8, :]
        send_ref[pl.ds(PARTS * y + 32, 8), :] = jnp.zeros((8, 128), F32)
        send_ref[pl.ds(PARTS * y + 40, 8), :] = small_ref[2 * (UNIT - 1) + y, 8:16, :]
    for block in range(UNIT):
        face_ref[pl.ds(8 * block, 8), :] = small_ref[2 * block + 1, 16:24, :]


def wells_kernel(recv_ref, held_ref, wx_ref, wy_ref, seg_ref, well_ref, term_ref):
    unit, here, after, before = places()
    own = iota((16, 128), 0) // 2
    groups = []
    for array in range(4):
        halves = []
        for y in range(2):
            whole = jnp.zeros((16, 128), F32)
            for owner in range(-UNIT, UNIT):
                base = here + 8 * owner if owner >= 0 else before + 8 * (owner + UNIT)
                place = UNIT - 1 - owner
                moved = lifted(rows_at(recv_ref, base + PARTS * y), 2 * place - 2 * array)
                whole = jnp.where(own == place, moved, whole)
            halves.append(whole)
        groups.append(jnp.concatenate(halves, axis=0))
    host, index, cond, rate = groups
    fm = jnp.where(iota(cond.shape, 1) > 0, cond, F32(0.0))
    well_ref[0], well_ref[1], well_ref[2], well_ref[3] = host, index, fm, rate
    zero = jnp.zeros(cond.shape, F32)
    seg = well_update(rate, index, fm, zero, zero)
    seg_ref[...] = seg
    spread_wells(F32(0.0) - index * seg, host, held_ref, term_ref)
    wy_ref[...] = recv_ref[4 * PARTS : 4 * PARTS + 32, :]
    for y in range(2):
        west = rows_at(recv_ref, before + PARTS * y + 40)
        wx_ref[y] = jnp.where(unit == 0, F32(0.0), west)


def first_kernel(
    shared_ref, wx_ref, wy_ref, held_ref, term_ref, p_ref, tx_out, ty_out, tz_out, gain_out, base_out, send_ref, face_ref,
    fields_ref, sem,
):
    members = 2 * UNIT
    loads = [
        pltpu.make_async_copy(shared_ref.at[m, pl.ds(0, 320)], fields_ref.at[m], sem.at[m]) for m in range(members)
    ]
    for load in loads:
        load.start()
    hots = [lane_onehot(held_ref[2 * block + y], 128) for y in range(2) for block in range(UNIT)]
    top = iota((8, 128), 1) == 127
    for x in range(32):
        if x % 8 == 0:
            loads[x // 4].wait()
            loads[x // 4 + 1].wait()
        for y in range(2):
            tx, ty, tz = (field(fields_ref, which, y, x) for which in (2, 3, 4))
            edge = field(fields_ref, 3, 0, x)[7:8, :] if y else wy_ref[x : x + 1, :]
            wx = field(fields_ref, 2, y, x - 1) if x else wx_ref[y]
            wy = y_moved(ty, edge, -1)
            inner = jnp.where(top, F32(0.0), tz)
            wz = pltpu.roll(inner, 1, 1)
            gain = F32(0.7) / (field(fields_ref, 1, y, x) + tx + wx + ty + wy + tz + wz)
            base = gain * field(fields_ref, 0, y, x)
            at = 32 * y + x
            tx_out[at], ty_out[at], tz_out[at], gain_out[at], base_out[at] = tx, ty, inner, gain, base
            p_ref[at] = base - gain * term_ref[at]
    send_out(p_ref, held_ref, hots, send_ref, face_ref)


def sweep_kernel(
    p_in, tx_ref, ty_ref, tz_ref, gain_ref, base_ref, wx_ref, wy_ref, recv_ref, seg_in, well_ref, held_ref, *rest, last
):
    if last:
        out_ref, seg_out = rest
    else:
        p_ref, seg_ref, send_ref, face_ref, term_ref = rest
    unit, here, after, before = places()
    units = lax.axis_size("gx") // UNIT
    host, index, fm, rate = well_ref[0], well_ref[1], well_ref[2], well_ref[3]
    own = iota((16, 128), 0) // 2
    halves = []
    for y in range(2):
        cell = jnp.zeros((16, 128), F32)
        near_host = host[16 * y : 16 * y + 16]
        for block in range(1 - UNIT, 2 * UNIT - 1):
            base = here if 0 <= block < UNIT else after if block > 0 else before
            vals = rows_at(recv_ref, base + PARTS * y + 8 * (block % UNIT))
            hit = near_host == (own + block - 3).astype(F32)
            cell = jnp.where(hit, lifted(vals, 6 - 2 * block), cell)
        halves.append(cell)
    cell_p = jnp.concatenate(halves, axis=0)
    seg = well_update(rate, index, fm, seg_in[...], cell_p)
    flux = index * (cell_p - seg)
    half = 4 * PARTS + 32
    lines = (slice(4 * PARTS, half), slice(half + 4 * PARTS, 2 * half))

    def updated(y, x, term):
        at = 32 * y + x
        block = p_in[at]
        if y:
            south, north = p_in[x, 7:8, :], recv_ref[lines[1].start + x : lines[1].start + x + 1, :]
        else:
            south, north = recv_ref[lines[0].start + x : lines[0].start + x + 1, :], p_in[32 + x, 0:1, :]
        if x < 31:
            east = p_in[at + 1]
        else:
            east = rows_at(recv_ref, after + PARTS * y + 32)
            east = jnp.where(unit == units - 1, F32(0.0), east)
        if x:
            west = p_in[at - 1]
        else:
            west = rows_at(recv_ref, before + PARTS * y + 40)
            west = jnp.where(unit == 0, F32(0.0), west)
        tx, ty, tz = tx_ref[at], ty_ref[at], tz_ref[at]
        edge = ty_ref[x, 7:8, :] if y else wy_ref[x : x + 1, :]
        total = tx * east + (tx_ref[at - 1] if x else wx_ref[y]) * west
        total = total + ty * y_moved(block, north, 1) + y_moved(ty, edge, -1) * y_moved(block, south, -1)
        total = total + tz * pltpu.roll(block, 127, 1) + pltpu.roll(tz, 1, 1) * pltpu.roll(block, 1, 1)
        return F32(0.3) * block + base_ref[at] + gain_ref[at] * (total - term)

    if last:
        place = lax.axis_index("gx") % UNIT
        core = lax.axis_index("gy") & 1
        for y in range(2):
            for block in range(UNIT):

                @pl.when((place == block) & (core == y))
                def _(y=y, block=block):
                    term, _ = spread_block(flux, host, held_ref, y, block)
                    for x in range(8):
                        out_ref[x] = updated(y, 8 * block + x, term[8 * x : 8 * x + 8])
                    start = 16 * y + 2 * (UNIT - 1 - block)
                    seg_out[0] = seg[start : start + 2]

    else:
        hots = spread_wells(flux, host, held_ref, term_ref)
        for y in range(2):
            for x in range(32):
                p_ref[32 * y + x] = updated(y, x, term_ref[32 * y + x])
        seg_ref[...] = seg
        send_out(p_ref, held_ref, hots, send_ref, face_ref)


def shards(
    rhs_field,
    accumulation,
    trans_x,
    trans_y,
    trans_z,
    held_cells,
    perf_host,
    well_index,
    seg_cond,
    seg_rate,
):
    ring = lax.axis_size("gx")
    county = lax.axis_size("gy")
    units = ring // UNIT
    facing = [(j, j + 1) for j in range(1, county - 1, 2)]
    facing += [(target, source) for source, target in facing]
    mates = [[j, j + 1] for j in range(0, county, 2)]
    chips = [
        [(UNIT * unit + x) * county + j + core for x in range(UNIT) for core in range(2)]
        for unit in range(units)
        for j in range(0, county, 2)
    ]
    columns = [
        [(((low + step + j % 2) % units) * UNIT + x) * county + j for step in range(2)]
        for j in range(county)
        for low in range(0, units, 2)
        for x in range(UNIT)
    ]

    def shape(*dims):
        return pltpu.VMEM(dims, F32)

    def result(*dims):
        return jax.ShapeDtypeStruct(dims, F32)

    def near(value):
        return pltpu.with_memory_space_constraint(value, pltpu.VMEM)

    vmem = pl.BlockSpec(memory_space=pltpu.VMEM)

    def call(body, outs, *args, placed=near, scratch=(), specs=None, **static):
        return pl.pallas_call(
            lambda *refs: body(*refs, **static),
            out_shape=outs,
            in_specs=[vmem] * len(args) if specs is None else specs,
            out_specs=[vmem] * len(outs),
            scratch_shapes=scratch,
        )(*map(placed, args))

    def exchanged(send, face):
        edge = lax.ppermute(face, "gy", facing)
        pair = lax.all_gather(send, ("gx", "gy"), axis_index_groups=columns, tiled=True)
        both = jnp.concatenate([pair, edge], axis=0)
        return lax.all_gather(both, "gy", axis_index_groups=mates, tiled=True)

    def among_chips(buffer):
        return lax.all_to_all(buffer, ("gx", "gy"), 0, 0, tiled=True, axis_index_groups=chips)

    small, large = call(
        pack_kernel, [result(8, 32, 128), result(8, 328, 128)], rhs_field, accumulation, trans_x, trans_y, trans_z,
        held_cells, perf_host, well_index, seg_cond, seg_rate, placed=lambda value: value,
    )
    fields = among_chips(large)
    message, edges, grid, wells = shape(96, 128), shape(32, 128), shape(64, 8, 128), shape(32, 128)
    send, face, held = call(
        share_kernel, [message, edges, pltpu.VMEM((8, 8, 128), jnp.int32)], among_chips(small)
    )
    recv = exchanged(send, face)
    wx, wy, seg, well, term = call(
        wells_kernel, [shape(2, 8, 128), edges, wells, shape(4, 32, 128), grid], recv, held
    )
    p, *kept, send, face = call(
        first_kernel, [grid] * 6 + [message, edges], fields, wx, wy, held, term,
        placed=lambda value: value if value is fields else near(value),
        specs=[pl.BlockSpec(memory_space=pl.ANY)] + [vmem] * 4,
        scratch=[shape(8, 320, 128), pltpu.SemaphoreType.DMA((8,))],
    )
    kept += [wx, wy]
    for sweep in range(1, SWEEPS):
        last = sweep == SWEEPS - 1
        recv = exchanged(send, face)
        outs = [result(8, 8, 128), result(1, 2, 128)] if last else [grid, wells, message, edges]
        got = call(
            sweep_kernel, outs, p, *kept, recv, seg, well, held, scratch=[] if last else [grid], last=last,
        )
        p, seg = got[:2]
        if not last:
            send, face = got[2:]
    return (p, seg)


def solution(mesh):
    return jax.shard_map(
        shards,
        mesh=mesh,
        in_specs=(
            P("gx", "gy", None),
            P("gx", "gy", None),
            P("gx", "gy", None),
            P("gx", "gy", None),
            P("gx", "gy", None),
            P(None, "gx", "gy", None),
            P("gx", "gy", None),
            P("gx", "gy", None),
            P("gx", "gy", None),
            P("gx", "gy", None),
        ),
        out_specs=(P("gx", "gy", None), P("gx", "gy", None)),
        check_vma=False,
    )
```

```python
import jax
import jax.numpy as jnp
from jax import lax
from jax.experimental import pallas as pl
from jax.experimental.pallas import tpu as pltpu
from jax.sharding import PartitionSpec as P

SWEEPS = 6
F32 = jnp.float32
BF16 = jnp.bfloat16


def split(value):
    high = value.astype(BF16)
    return high, (value - high.astype(F32)).astype(BF16)


def iota(shape, dim):
    return lax.broadcasted_iota(jnp.int32, shape, dim)


def lane_onehot(idx, lanes):
    lane_of = idx & (lanes - 1)
    pieces = []
    for row in range(idx.shape[0]):
        hit = iota((lanes, idx.shape[1]), 0) == lane_of[row : row + 1, :]
        pieces.append(jnp.where(hit, F32(1.0), F32(0.0)).astype(BF16))
    return jnp.concatenate(pieces, axis=1)


def row_hit(idx, row, lanes, count):
    shift = lanes.bit_length() - 1
    row_of = lax.shift_right_logical(idx[row : row + 1, :], shift)
    return iota((count, idx.shape[1]), 0) == row_of


def scatter(flux, idx, lane_hot, count, lanes):
    parts = [part.astype(F32) for part in split(flux)]
    columns = []
    for row in range(idx.shape[0]):
        hit = row_hit(idx, row, lanes, count)
        columns.append(
            jnp.concatenate(
                [jnp.where(hit, part[row : row + 1, :], F32(0.0)).astype(BF16) for part in parts],
                axis=0,
            )
        )
    spread = jnp.concatenate(columns, axis=1)
    out = lax.dot_general(
        spread, lane_hot, (((1,), (1,)), ((), ())), preferred_element_type=F32
    )
    return out[:count] + out[count:]


def gather(cells, idx, lane_hot, lanes):
    count = cells.shape[0]
    stacked = jnp.concatenate(split(cells), axis=0)
    picked = lax.dot_general(
        stacked, lane_hot, (((1,), (0,)), ((), ())), preferred_element_type=F32
    )
    picked = picked[:count] + picked[count:]
    slots = idx.shape[1]
    out = jnp.zeros(idx.shape, F32)
    for row in range(idx.shape[0]):
        part = jnp.where(
            row_hit(idx, row, lanes, count), picked[:, row * slots : (row + 1) * slots], F32(0.0)
        )
        total = jnp.sum(part, axis=0, keepdims=True)
        out = jnp.where(iota(idx.shape, 0) == row, total, out)
    return out


def well_update(rate, index, fm, seg, cell_p):
    slots = seg.shape[1]
    fp = pltpu.roll(fm, slots - 1, 1)
    seg_prev = pltpu.roll(seg, 1, 1)
    seg_next = pltpu.roll(seg, slots - 1, 1)
    seg_res = rate - (
        index * (seg - cell_p) + fm * (seg - seg_prev) + fp * (seg - seg_next)
    )
    return seg + F32(0.8) * seg_res / (index + fm + fp)


UNIT = 4
PARTS = 48


def z_shifted(plane, step):
    size = plane.shape[1]
    moved = pltpu.roll(plane, (-step) % size, 1)
    at = size - 1 if step > 0 else 0
    return jnp.where(iota(plane.shape, 1) == at, F32(0.0), moved)


def y_moved(plane, edge, step):
    size = plane.shape[0]
    at = size - 1 if step > 0 else 0
    return jnp.where(iota(plane.shape, 0) == at, edge, pltpu.roll(plane, (-step) % size, 0))


def places():
    unit = lax.axis_index("gx") // UNIT
    odd = unit & 1
    half = 4 * PARTS + 8 * UNIT
    return unit, odd * 2 * PARTS, odd * half + 2 * PARTS, (1 - odd) * half


def rows_at(recv_ref, start, count=8):
    return recv_ref[pl.ds(pl.multiple_of(start, 8), count), :]


def lifted(piece, shift):
    tall = jnp.concatenate([piece, jnp.zeros_like(piece)], axis=0)
    shift = shift % tall.shape[0]
    return pltpu.roll(tall, shift, 0) if shift else tall


def window(rows, y, block):
    start = 16 * y + 6 - 2 * block
    moved = pltpu.roll(rows, (-start) % rows.shape[0], 0) if start else rows
    return moved[:8]


def spread_block(flux, host, held_ref, y, block):
    near_host = window(host, y, block)
    part = window(flux, y, block)
    part = jnp.where(near_host == (iota(part.shape, 0) // 2).astype(F32), part, F32(0.0))
    idx = held_ref[2 * block + y]
    hot = lane_onehot(idx, 128)
    return scatter(part, idx, hot, 64, 128), hot


def spread_wells(flux, host, held_ref, term_ref):
    hots = []
    for y in range(2):
        for block in range(UNIT):
            term, hot = spread_block(flux, host, held_ref, y, block)
            hots.append(hot)
            term_ref[pl.ds(32 * y + 8 * block, 8)] = term.reshape(8, 8, 128)
    return hots


def send_out(p_ref, held_ref, hots, send_ref, face_ref):
    for y in range(2):
        for block in range(UNIT):
            cells = p_ref[pl.ds(32 * y + 8 * block, 8)].reshape(64, 128)
            vals = gather(cells, held_ref[2 * block + y], hots[UNIT * y + block], 128)
            send_ref[pl.ds(PARTS * y + 8 * block, 8), :] = vals
        send_ref[pl.ds(PARTS * y + 32, 8), :] = p_ref[32 * y]
        send_ref[pl.ds(PARTS * y + 40, 8), :] = p_ref[32 * y + 31]
    upper = (lax.axis_index("gy") & 1) == 1
    for x in range(32):
        face_ref[x : x + 1, :] = jnp.where(upper, p_ref[32 + x, 7:8, :], p_ref[x, 0:1, :])


def field(fields_ref, which, y, x):
    return fields_ref[2 * (x // 8) + y, pl.ds(64 * which + 8 * (x % 8), 8), :]


def pack_kernel(
    rhs_ref, acc_ref, tx_ref, ty_ref, tz_ref, held_ref, host_ref, index_ref, cond_ref, rate_ref, small_ref, large_ref,
    whole_ref, sem
):
    members = large_ref.shape[0]
    for which, ref in enumerate((rhs_ref, acc_ref, tx_ref, ty_ref, tz_ref)):
        whole_ref[64 * which : 64 * which + 64, :] = ref[...].reshape(64, 128)
    whole_ref[320:328, :] = held_ref[...].reshape(8, 128).astype(F32)
    copies = [pltpu.make_async_copy(whole_ref, large_ref.at[m], sem.at[m]) for m in range(members)]
    for copy in copies:
        copy.start()
    pack = jnp.concatenate(
        [host_ref[0].astype(F32), index_ref[0], cond_ref[0], rate_ref[0]], axis=0
    )
    edge = jnp.concatenate([ty_ref[x, 7:8, :] for x in range(8)], axis=0)
    for m in range(members):
        small_ref[m, 0:8, :] = pack
        small_ref[m, 8:16, :] = tx_ref[7]
        small_ref[m, 16:24, :] = edge
    for copy in copies:
        copy.wait()


def share_kernel(small_ref, send_ref, face_ref):
    for y in range(2):
        for block in range(UNIT):
            send_ref[pl.ds(PARTS * y + 8 * block, 8), :] = small_ref[2 * block + y, 0:8, :]
        send_ref[pl.ds(PARTS * y + 32, 8), :] = jnp.zeros((8, 128), F32)
        send_ref[pl.ds(PARTS * y + 40, 8), :] = small_ref[2 * (UNIT - 1) + y, 8:16, :]
    for block in range(UNIT):
        face_ref[pl.ds(8 * block, 8), :] = small_ref[2 * block + 1, 16:24, :]


def first_kernel(
    shared_ref, recv_ref, p_ref, tx_out, ty_out, tz_out, gain_out, base_out, wx_ref, wy_ref, seg_ref, well_ref, held_ref, send_ref, face_ref, term_ref, fields_ref, sem
):
    tail, body = pl.ds(320, 8), pl.ds(0, 320)
    late = pltpu.make_async_copy(shared_ref.at[:, tail], fields_ref.at[:, tail], sem.at[0])
    main = pltpu.make_async_copy(shared_ref.at[:, body], fields_ref.at[:, body], sem.at[1])
    late.start()
    main.start()
    unit, here, after, before = places()
    own = iota((16, 128), 0) // 2
    groups = []
    for array in range(4):
        halves = []
        for y in range(2):
            whole = jnp.zeros((16, 128), F32)
            for owner in range(-UNIT, UNIT):
                base = here + 8 * owner if owner >= 0 else before + 8 * (owner + UNIT)
                place = UNIT - 1 - owner
                moved = lifted(rows_at(recv_ref, base + PARTS * y), 2 * place - 2 * array)
                whole = jnp.where(own == place, moved, whole)
            halves.append(whole)
        groups.append(jnp.concatenate(halves, axis=0))
    host, index, cond, rate = groups
    fm = jnp.where(iota(cond.shape, 1) > 0, cond, F32(0.0))
    well_ref[0], well_ref[1], well_ref[2], well_ref[3] = host, index, fm, rate
    zero = jnp.zeros(cond.shape, F32)
    seg = well_update(rate, index, fm, zero, zero)
    seg_ref[...] = seg
    late.wait()
    for m in range(2 * UNIT):
        held_ref[m] = fields_ref[m, 320:328, :].astype(jnp.int32)
    hots = spread_wells(F32(0.0) - index * seg, host, held_ref, term_ref)
    wy_ref[...] = recv_ref[4 * PARTS : 4 * PARTS + 32, :]
    main.wait()
    top = iota((8, 128), 1) == 127
    for y in range(2):
        west = rows_at(recv_ref, before + PARTS * y + 40)
        west = jnp.where(unit == 0, F32(0.0), west)
        wx_ref[y] = west
        for x in range(32):
            tx, ty, tz = (field(fields_ref, which, y, x) for which in (2, 3, 4))
            edge = field(fields_ref, 3, 0, x)[7:8, :] if y else recv_ref[4 * PARTS + x : 4 * PARTS + x + 1, :]
            wx = field(fields_ref, 2, y, x - 1) if x else west
            wy = y_moved(ty, edge, -1)
            inner = jnp.where(top, F32(0.0), tz)
            wz = pltpu.roll(inner, 1, 1)
            gain = F32(0.7) / (field(fields_ref, 1, y, x) + tx + wx + ty + wy + tz + wz)
            base = gain * field(fields_ref, 0, y, x)
            at = 32 * y + x
            tx_out[at], ty_out[at], tz_out[at], gain_out[at], base_out[at] = tx, ty, inner, gain, base
            p_ref[at] = base - gain * term_ref[at]
    send_out(p_ref, held_ref, hots, send_ref, face_ref)


def sweep_kernel(
    p_in, tx_ref, ty_ref, tz_ref, gain_ref, base_ref, wx_ref, wy_ref, recv_ref, seg_in, well_ref, held_ref, *rest, last
):
    if last:
        out_ref, seg_out = rest
    else:
        p_ref, seg_ref, send_ref, face_ref, term_ref = rest
    unit, here, after, before = places()
    units = lax.axis_size("gx") // UNIT
    host, index, fm, rate = well_ref[0], well_ref[1], well_ref[2], well_ref[3]
    own = iota((16, 128), 0) // 2
    halves = []
    for y in range(2):
        cell = jnp.zeros((16, 128), F32)
        near_host = host[16 * y : 16 * y + 16]
        for block in range(1 - UNIT, 2 * UNIT - 1):
            base = here if 0 <= block < UNIT else after if block > 0 else before
            vals = rows_at(recv_ref, base + PARTS * y + 8 * (block % UNIT))
            hit = near_host == (own + block - 3).astype(F32)
            cell = jnp.where(hit, lifted(vals, 6 - 2 * block), cell)
        halves.append(cell)
    cell_p = jnp.concatenate(halves, axis=0)
    seg = well_update(rate, index, fm, seg_in[...], cell_p)
    flux = index * (cell_p - seg)
    half = 4 * PARTS + 32
    lines = (slice(4 * PARTS, half), slice(half + 4 * PARTS, 2 * half))

    def updated(y, x, term):
        at = 32 * y + x
        block = p_in[at]
        if y:
            south, north = p_in[x, 7:8, :], recv_ref[lines[1].start + x : lines[1].start + x + 1, :]
        else:
            south, north = recv_ref[lines[0].start + x : lines[0].start + x + 1, :], p_in[32 + x, 0:1, :]
        if x < 31:
            east = p_in[at + 1]
        else:
            east = rows_at(recv_ref, after + PARTS * y + 32)
            east = jnp.where(unit == units - 1, F32(0.0), east)
        if x:
            west = p_in[at - 1]
        else:
            west = rows_at(recv_ref, before + PARTS * y + 40)
            west = jnp.where(unit == 0, F32(0.0), west)
        tx, ty, tz = tx_ref[at], ty_ref[at], tz_ref[at]
        edge = ty_ref[x, 7:8, :] if y else wy_ref[x : x + 1, :]
        total = tx * east + (tx_ref[at - 1] if x else wx_ref[y]) * west
        total = total + ty * y_moved(block, north, 1) + y_moved(ty, edge, -1) * y_moved(block, south, -1)
        total = total + tz * pltpu.roll(block, 127, 1) + pltpu.roll(tz, 1, 1) * pltpu.roll(block, 1, 1)
        return F32(0.3) * block + base_ref[at] + gain_ref[at] * (total - term)

    if last:
        place = lax.axis_index("gx") % UNIT
        core = lax.axis_index("gy") & 1
        for y in range(2):
            for block in range(UNIT):

                @pl.when((place == block) & (core == y))
                def _(y=y, block=block):
                    term, _ = spread_block(flux, host, held_ref, y, block)
                    for x in range(8):
                        out_ref[x] = updated(y, 8 * block + x, term[8 * x : 8 * x + 8])
                    start = 16 * y + 2 * (UNIT - 1 - block)
                    seg_out[0] = seg[start : start + 2]

    else:
        hots = spread_wells(flux, host, held_ref, term_ref)
        for y in range(2):
            for x in range(32):
                p_ref[32 * y + x] = updated(y, x, term_ref[32 * y + x])
        seg_ref[...] = seg
        send_out(p_ref, held_ref, hots, send_ref, face_ref)


def shards(
    rhs_field,
    accumulation,
    trans_x,
    trans_y,
    trans_z,
    held_cells,
    perf_host,
    well_index,
    seg_cond,
    seg_rate,
):
    ring = lax.axis_size("gx")
    county = lax.axis_size("gy")
    units = ring // UNIT
    facing = [(j, j + 1) for j in range(1, county - 1, 2)]
    facing += [(target, source) for source, target in facing]
    mates = [[j, j + 1] for j in range(0, county, 2)]
    chips = [
        [(UNIT * unit + x) * county + j + core for x in range(UNIT) for core in range(2)]
        for unit in range(units)
        for j in range(0, county, 2)
    ]
    columns = [
        [(((low + step + j % 2) % units) * UNIT + x) * county + j for step in range(2)]
        for j in range(county)
        for low in range(0, units, 2)
        for x in range(UNIT)
    ]

    def shape(*dims):
        return pltpu.VMEM(dims, F32)

    def result(*dims):
        return jax.ShapeDtypeStruct(dims, F32)

    def near(value):
        return pltpu.with_memory_space_constraint(value, pltpu.VMEM)

    vmem = pl.BlockSpec(memory_space=pltpu.VMEM)

    def call(body, outs, *args, placed=near, scratch=(), specs=None, places_out=None, **static):
        return pl.pallas_call(
            lambda *refs: body(*refs, **static),
            out_shape=outs,
            in_specs=[vmem] * len(args) if specs is None else specs,
            out_specs=[vmem] * len(outs) if places_out is None else places_out,
            scratch_shapes=scratch,
        )(*map(placed, args))

    def exchanged(send, face):
        edge = lax.ppermute(face, "gy", facing)
        pair = lax.all_gather(send, ("gx", "gy"), axis_index_groups=columns, tiled=True)
        both = jnp.concatenate([pair, edge], axis=0)
        return lax.all_gather(both, "gy", axis_index_groups=mates, tiled=True)

    def among_chips(buffer):
        return lax.all_to_all(buffer, ("gx", "gy"), 0, 0, tiled=True, axis_index_groups=chips)

    small, large = call(
        pack_kernel, [result(8, 24, 128), result(8, 328, 128)], rhs_field, accumulation, trans_x, trans_y, trans_z,
        held_cells, perf_host, well_index, seg_cond, seg_rate, placed=lambda value: value,
        places_out=[vmem, pl.BlockSpec(memory_space=pl.ANY)],
        scratch=[shape(328, 128), pltpu.SemaphoreType.DMA((8,))],
    )
    fields = among_chips(large)
    message, edges, grid, wells = shape(96, 128), shape(32, 128), shape(64, 8, 128), shape(32, 128)
    send, face = call(share_kernel, [message, edges], among_chips(small))
    recv = exchanged(send, face)
    p, *kept, seg, well, held, send, face = call(
        first_kernel,
        [grid] * 6 + [shape(2, 8, 128), edges, wells, shape(4, 32, 128), pltpu.VMEM((8, 8, 128), jnp.int32), message, edges],
        fields, recv, scratch=[grid, shape(8, 328, 128), pltpu.SemaphoreType.DMA((2,))],
        specs=[pl.BlockSpec(memory_space=pl.ANY), vmem], placed=lambda value: value if value is fields else near(value),
    )
    for sweep in range(1, SWEEPS):
        last = sweep == SWEEPS - 1
        recv = exchanged(send, face)
        outs = [result(8, 8, 128), result(1, 2, 128)] if last else [grid, wells, message, edges]
        got = call(
            sweep_kernel, outs, p, *kept, recv, seg, well, held, scratch=[] if last else [grid], last=last,
        )
        p, seg = got[:2]
        if not last:
            send, face = got[2:]
    return (p, seg)


def solution(mesh):
    return jax.shard_map(
        shards,
        mesh=mesh,
        in_specs=(
            P("gx", "gy", None),
            P("gx", "gy", None),
            P("gx", "gy", None),
            P("gx", "gy", None),
            P("gx", "gy", None),
            P(None, "gx", "gy", None),
            P("gx", "gy", None),
            P("gx", "gy", None),
            P("gx", "gy", None),
            P("gx", "gy", None),
        ),
        out_specs=(P("gx", "gy", None), P("gx", "gy", None)),
        check_vma=False,
    )
```
